32 devices in a mesh: dp: 4 (over x, core), fsdp: 4 (over z), ctx: 2 (over y).
Axes of the slice: x: 2, y: 2, z: 4, core: 2. Of those that a mesh axis runs over, the one named last changes fastest.
Arguments:
- tokens: bfloat16 [16, 1024, 768], P(('dp', 'fsdp'), 'ctx'), may hold values from -6 to 6
- cotangent: bfloat16 [16, 1024, 768], P(('dp', 'fsdp'), 'ctx'), may hold values from -6 to 6
- w_qkv: bfloat16 [768, 2304], P('fsdp'), may hold values from -0.21875 to 0.21875
- w_forget: bfloat16 [768, 12], P('fsdp'), may hold values from -0.4375 to 0.4375
- w_ogate: bfloat16 [768, 768], P('fsdp'), may hold values from -0.21875 to 0.21875
- w_out: bfloat16 [768, 768], P('fsdp'), may hold values from -3 to 3
- w_gu: bfloat16 [768, 4096], P('fsdp'), may hold values from -0.21875 to 0.21875
- w_down: bfloat16 [2048, 768], P('fsdp'), may hold values from -0.125 to 0.125
- norm_attn: float32 [768], replicated, may hold values from 0.1 to 1.9
- norm_ffn: float32 [768], replicated, may hold values from 0.1 to 1.9
- query_gain: float32 [64], replicated, may hold values from 0.1 to 1.9
- key_gain: float32 [64], replicated, may hold values from 0.1 to 1.9
- forget_bias: float32 [12], replicated, may hold values from 5.5 to 9.5
- ogate_bias: float32 [768], replicated, may hold values from -4 to 4
Outputs:
- out: float32 [16, 1024, 768], P(('dp', 'fsdp'), 'ctx')
- d_tokens: float32 [16, 1024, 768], P(('dp', 'fsdp'), 'ctx')
- grad_qkv: float32 [768, 2304], P('fsdp')
- grad_forget: float32 [768, 12], P('fsdp')
- grad_ogate: float32 [768, 768], P('fsdp')
- grad_out: float32 [768, 768], P('fsdp')
- grad_gu: float32 [768, 4096], P('fsdp')
- grad_down: float32 [2048, 768], P('fsdp')
- grad_norm_attn: float32 [768], replicated
- grad_norm_ffn: float32 [768], replicated
- grad_query_gain: float32 [64], replicated
- grad_key_gain: float32 [64], replicated
- grad_forget_bias: float32 [12], replicated
- grad_ogate_bias: float32 [768], replicated
The draws below stay inside these ranges and needn't reach their ends.
All inputs are finite; a program needn't handle non-finite values.
Results may differ from the reference program's by a relative error of at most 0.01895.
Values may be sent and summed in bfloat16 or wider, within the bound.
A program may use at most 192 MiB of HBM per device.

```python
import jax
import jax.numpy as jnp
from jax import lax

D = 768
H = 12
HD = 64
FF = 2048
SEQ_LEN = 1024
NSEQ = 16


def draw_forget_bias(key, part):
    values = jax.random.uniform(key, (H,), jnp.float32, 5.5, 8.5)
    return values


def levels(key, extent, cuts, low, largest):
    def one(dim, shards_of):
        draws = jax.random.uniform(jax.random.fold_in(jax.random.fold_in(key, 6), dim), (shards_of,), jnp.float32, low / len(cuts), largest / len(cuts))
        return jnp.repeat(jnp.exp(draws), extent[dim] // shards_of).reshape((-1,) + (1,) * (len(extent) - dim - 1))

    loudness = one(*cuts[0])
    for cut in cuts[1:]:
        loudness = loudness * one(*cut)
    return loudness


def centred(key, extent, deviation, most, split=(), dtype=jnp.bfloat16):
    entries = deviation * jax.random.normal(key, extent, jnp.float32)
    if split:
        entries = entries * levels(key, extent, split, -0.22, 0.18)
    return jnp.clip(entries, -most, most).astype(dtype)


def setup_inputs(seed: int = 0) -> dict:
    key_list = jax.random.split(jax.random.key(seed), 15)
    return {
        "tokens": centred(key_list[0], (NSEQ, SEQ_LEN, D), 1.0, 6.0, ((0, 16), (1, 2))),
        "cotangent": centred(key_list[1], (NSEQ, SEQ_LEN, D), 1.0, 6.0, ((0, 16), (1, 2))),
        "w_qkv": centred(key_list[2], (D, 3 * D), D ** -0.5, 0.21875, ((0, 4),)),
        "w_forget": centred(key_list[3], (D, H), (D // 4) ** -0.5, 0.4375, ((0, 4),)),
        "w_ogate": centred(key_list[4], (D, D), D ** -0.5, 0.21875, ((0, 4),)),
        "w_out": centred(key_list[5], (D, D), 4 ** -0.5, 3.0, ((0, 4),)),
        "w_gu": centred(key_list[6], (D, 2 * FF), D ** -0.5, 0.21875, ((0, 4),)),
        "w_down": centred(key_list[7], (FF, D), FF ** -0.5, 0.125, ((0, 4),)),
        "norm_attn": jnp.clip(1.0 + 0.18 * jax.random.normal(key_list[8], (D,), jnp.float32), 0.1, 1.9),
        "norm_ffn": jnp.clip(1.0 + 0.18 * jax.random.normal(key_list[9], (D,), jnp.float32), 0.1, 1.9),
        "query_gain": jnp.clip(1.0 + 0.18 * jax.random.normal(key_list[10], (HD,), jnp.float32), 0.1, 1.9),
        "key_gain": jnp.clip(1.0 + 0.18 * jax.random.normal(key_list[11], (HD,), jnp.float32), 0.1, 1.9),
        "forget_bias": draw_forget_bias(jax.random.fold_in(key_list[14], 71), 0),
        "ogate_bias": centred(key_list[13], (D,), 1.0, 4.0, (), jnp.float32),
    }


@jax.custom_vjp
def low(v):
    return lax.optimization_barrier(v.astype(jnp.bfloat16)).astype(jnp.float32)

@jax.custom_vjp
def low_back(v):
    return v

def low_keep(v):
    return (low(v), None)

def low_pass(kept, grad):
    return (grad,)

def back_keep(v):
    return (v, None)

def back_low(kept, grad):
    return (low(grad),)
low.defvjp(low_keep, low_pass)
low_back.defvjp(back_keep, back_low)
EPS = 1e-06

def product(left, right):
    return jnp.dot(left, right, precision=lax.Precision.HIGHEST)

def norm_rows(values, gain):
    return values * lax.rsqrt(lax.optimization_barrier(jnp.mean(values * values, axis=-1, keepdims=True)) + EPS) * gain

def head_attention(pieces):
    query, keys, values, cum = pieces
    length = query.shape[0]
    scale = query.shape[1] ** (-0.5)
    logits = low_back(product(query, keys.T) * scale)
    scores = logits + cum[:, None] - cum[None, :]
    places = jnp.arange(length)
    allowed = places[None, :] <= places[:, None]
    scores = jnp.where(allowed, scores, -1e+30)
    probs = jax.nn.softmax(scores, axis=-1)
    return low_back(product(low(probs), values))

def layer(x, w_qkv, w_forget, w_ogate, w_out, w_gu, w_down, norm_attn, norm_ffn, query_gain, key_gain, forget_bias, ogate_bias):
    length, width = x.shape
    heads = forget_bias.shape[0]
    head_dim = query_gain.shape[0]
    hidden = w_down.shape[0]
    act_one = low(norm_rows(x, norm_attn))
    qkv = low_back(product(act_one, w_qkv))
    query = low(norm_rows(qkv[:, :width].reshape(length, heads, head_dim), query_gain))
    keys = low(norm_rows(qkv[:, width:2 * width].reshape(length, heads, head_dim), key_gain))
    values = low(qkv[:, 2 * width:].reshape(length, heads, head_dim))
    gate_pre = low_back(product(act_one, w_forget)) + forget_bias
    cum = jnp.cumsum(jax.nn.log_sigmoid(gate_pre), axis=0)
    attended = lax.map(jax.checkpoint(head_attention), (query.transpose(1, 0, 2), keys.transpose(1, 0, 2), values.transpose(1, 0, 2), cum.T))
    attn = attended.transpose(1, 0, 2).reshape(length, width)
    ogate = jax.nn.sigmoid(low_back(product(act_one, w_ogate)) + ogate_bias)
    gated = low(attn * ogate)
    middle = x + low_back(product(gated, w_out))
    act_two = low(norm_rows(middle, norm_ffn))
    gate_up = low_back(product(act_two, w_gu))
    hidden_low = low(jax.nn.silu(gate_up[:, :hidden]) * gate_up[:, hidden:])
    return middle + low_back(product(hidden_low, w_down))

def reference(tokens, cotangent, w_qkv, w_forget, w_ogate, w_out, w_gu, w_down, norm_attn, norm_ffn, query_gain, key_gain, forget_bias, ogate_bias):
    params = tuple((w.astype(jnp.float32) for w in (w_qkv, w_forget, w_ogate, w_out, w_gu, w_down, norm_attn, norm_ffn, query_gain, key_gain, forget_bias, ogate_bias)))
    inputs = tokens.astype(jnp.float32)
    grads_in = cotangent.astype(jnp.float32)

    def one(carry, pair):
        sequence, grad_seq = pair
        result, pull = jax.vjp(layer, sequence, *params)
        pulled = pull(grad_seq)
        return (tuple((c + g for c, g in zip(carry, pulled[1:]))), (result, pulled[0]))
    start = tuple((jnp.zeros(w.shape, jnp.float32) for w in params))
    sums, (results, grad_inputs) = lax.scan(one, start, (inputs, grads_in))
    return (results, grad_inputs, sums[0], sums[1], sums[2], sums[3], sums[4], sums[5], sums[6], sums[7], sums[8], sums[9], sums[10], sums[11])
```

```python
import jax
import jax.numpy as jnp
from jax import lax
from jax.sharding import PartitionSpec as P

EPS = 1e-06
NEG_FILL = -1e30


def prefix_2(array, axis, combine, identity, reverse):
    size, position = (lax.axis_size(axis), lax.axis_index(axis))
    everything = lax.all_gather(array, axis)
    start = jnp.broadcast_to(jnp.asarray(identity, array.dtype), array.shape)

    def lap(k, before):
        at = size - 1 - k if reverse else k
        reached = at > position if reverse else at < position
        new = combine(before, everything[at])
        return jnp.where(reached, new, before)

    return lax.fori_loop(0, size, lap, start)


def rms_factor(values):
    return lax.rsqrt(jnp.mean(values * values, axis=-1, keepdims=True) + EPS)


def rms_back(values, factor, grad_normed, gain):
    scaled = grad_normed * gain
    inner = jnp.mean(scaled * values, axis=-1, keepdims=True)
    return factor * scaled - factor * factor * factor * values * inner


def inner_rows(left, right):
    return lax.dot_general(
        left, right, (((0,), (0,)), ((), ())), preferred_element_type=jnp.float32
    )


def times_trans(left, right):
    return lax.dot_general(
        left, right, (((1,), (1,)), ((), ())), preferred_element_type=jnp.float32
    )


def add_terms(earlier, later):
    return earlier + later


def masked_scores(q_head, k_head, q_cum, k_cum, allowed, scale):
    logits = times_trans(q_head, k_head) * scale
    scores = logits + q_cum[:, None] - k_cum[None, :]
    return jnp.where(allowed, scores, NEG_FILL)


def gather_rows(local):
    part = local.shape[0] // (lax.axis_size("dp") * lax.axis_size("ctx"))
    rank = lax.axis_index("dp") * lax.axis_size("ctx") + lax.axis_index("ctx")
    piece = lax.dynamic_slice_in_dim(local, rank * part, part, axis=0)
    return lax.all_gather(piece, ("fsdp", "dp", "ctx"), axis=0, tiled=True)


def reduce_rows(grad):
    piece = lax.psum_scatter(
        grad.astype(jnp.bfloat16), ("fsdp", "dp", "ctx"), scatter_dimension=0, tiled=True
    )
    return lax.all_gather(piece, ("dp", "ctx"), axis=0, tiled=True).astype(jnp.float32)


def shards(
    tokens,
    cotangent,
    w_qkv,
    w_forget,
    w_ogate,
    w_out,
    w_gu,
    w_down,
    norm_attn,
    norm_ffn,
    query_gain,
    key_gain,
    forget_bias,
    ogate_bias,
):
    inputs = tokens[0].astype(jnp.float32)
    grad_top = cotangent[0].astype(jnp.float32)
    rows, width = inputs.shape
    heads = forget_bias.shape[0]
    head_dim = query_gain.shape[0]
    hidden = w_gu.shape[1] // 2
    ctx_count = lax.axis_size("ctx")
    ctx_rank = lax.axis_index("ctx")
    key_rows = rows * ctx_count
    scale = head_dim ** (-0.5)
    local_weights = (w_qkv, w_forget, w_ogate, w_out, w_gu, w_down)
    gathered = tuple(gather_rows(piece) for piece in local_weights)
    qkv_full, forget_full, ogate_full, out_full, gu_full, down_full = gathered
    factor_one = rms_factor(inputs)
    act_one = (inputs * factor_one * norm_attn).astype(jnp.bfloat16)
    qkv = jnp.dot(act_one, qkv_full, preferred_element_type=jnp.float32)
    query = qkv[:, :width].reshape(rows, heads, head_dim)
    keys = qkv[:, width : 2 * width].reshape(rows, heads, head_dim)
    query_factor = rms_factor(query)
    key_factor = rms_factor(keys)
    query_low = (query * query_factor * query_gain).astype(jnp.bfloat16)
    key_low = (keys * key_factor * key_gain).astype(jnp.bfloat16)
    value_low = qkv[:, 2 * width :].astype(jnp.bfloat16)
    gate_pre = jnp.dot(act_one, forget_full, preferred_element_type=jnp.float32) + forget_bias
    local_cum = jnp.cumsum(jax.nn.log_sigmoid(gate_pre), axis=0).T
    last_flag = (jnp.arange(rows) == rows - 1).astype(jnp.float32)
    prefix = prefix_2(local_cum[:, -1], "ctx", add_terms, jnp.zeros((heads,), jnp.float32), False)
    sent_cum = local_cum + prefix[:, None]
    key_pair = (
        lax.all_gather(key_low.reshape(rows, width), "ctx", axis=0, tiled=True),
        lax.all_gather(value_low, "ctx", axis=0, tiled=True),
    )
    gathered_cum = lax.all_gather(sent_cum, "ctx", axis=1, tiled=True)
    key_heads = key_pair[0].reshape(key_rows, heads, head_dim).transpose(1, 0, 2)
    value_heads = key_pair[1].reshape(key_rows, heads, head_dim).transpose(1, 0, 2)
    query_heads = query_low.transpose(1, 0, 2)
    query_pos = ctx_rank * rows + jnp.arange(rows)
    allowed = jnp.arange(key_rows)[None, :] <= query_pos[:, None]

    def forward_head(pieces):
        q_head, k_head, v_head, q_cum, k_cum = pieces
        scores = masked_scores(q_head, k_head, q_cum, k_cum, allowed, scale)
        top = jnp.max(scores, axis=1, keepdims=True)
        expd = jnp.exp(scores - top)
        total = jnp.sum(expd, axis=1, keepdims=True)
        weights_low = (expd / total).astype(jnp.bfloat16)
        attended_head = jnp.dot(weights_low, v_head, preferred_element_type=jnp.float32)
        return (attended_head, (top + jnp.log(total))[:, 0])

    attended, log_total = lax.map(
        forward_head, (query_heads, key_heads, value_heads, sent_cum, gathered_cum)
    )
    attn = attended.transpose(1, 0, 2).reshape(rows, width)
    ogate = jax.nn.sigmoid(
        jnp.dot(act_one, ogate_full, preferred_element_type=jnp.float32) + ogate_bias
    )
    gated = (attn * ogate).astype(jnp.bfloat16)
    middle = inputs + jnp.dot(gated, out_full, preferred_element_type=jnp.float32)
    factor_two = rms_factor(middle)
    act_two = (middle * factor_two * norm_ffn).astype(jnp.bfloat16)
    gate_up = jnp.dot(act_two, gu_full, preferred_element_type=jnp.float32)
    gate_part = gate_up[:, :hidden]
    up_part = gate_up[:, hidden:]
    hidden_low = (jax.nn.silu(gate_part) * up_part).astype(jnp.bfloat16)
    result = middle + jnp.dot(hidden_low, down_full, preferred_element_type=jnp.float32)
    qkv_back, forget_back, ogate_back, out_back, gu_back, down_back = gathered
    grad_low = grad_top.astype(jnp.bfloat16)
    grad_down = inner_rows(hidden_low, grad_low)
    grad_hidden = times_trans(grad_low, down_back)
    sigma = jax.nn.sigmoid(gate_part)
    grad_gu_low = jnp.concatenate(
        [
            grad_hidden * up_part * sigma * (1.0 + gate_part * (1.0 - sigma)),
            grad_hidden * (gate_part * sigma),
        ],
        axis=1,
    ).astype(jnp.bfloat16)
    grad_gu = inner_rows(act_two, grad_gu_low)
    grad_act_two = times_trans(grad_gu_low, gu_back)
    grad_norm_ffn = jnp.sum(grad_act_two * middle * factor_two, axis=0)
    grad_middle = grad_top + rms_back(middle, factor_two, grad_act_two, norm_ffn)
    middle_low = grad_middle.astype(jnp.bfloat16)
    grad_out = inner_rows(gated, middle_low)
    grad_gated = times_trans(middle_low, out_back)
    grad_attn_low = (grad_gated * ogate).astype(jnp.bfloat16)
    grad_ogate_pre = grad_gated * attn * ogate * (1.0 - ogate)
    grad_ogate_bias = jnp.sum(grad_ogate_pre, axis=0)
    ogate_low = grad_ogate_pre.astype(jnp.bfloat16)
    grad_attn_heads = grad_attn_low.reshape(rows, heads, head_dim).transpose(1, 0, 2)

    def backward_head(pieces):
        q_head, k_head, v_head, q_cum, k_cum, total_log, grad_head = pieces
        scores = masked_scores(q_head, k_head, q_cum, k_cum, allowed, scale)
        probs = jnp.exp(scores - total_log[:, None])
        grad_probs = times_trans(grad_head, v_head)
        grad_value = inner_rows(probs.astype(jnp.bfloat16), grad_head)
        grad_scores = probs * (grad_probs - jnp.sum(probs * grad_probs, axis=1, keepdims=True))
        scores_low = grad_scores.astype(jnp.bfloat16)
        grad_query = jnp.dot(scores_low, k_head, preferred_element_type=jnp.float32) * scale
        grad_key = inner_rows(scores_low, q_head) * scale
        return (
            grad_query,
            grad_key,
            grad_value,
            jnp.sum(grad_scores, axis=1),
            -jnp.sum(grad_scores, axis=0),
        )

    grad_q, grad_k_heads, grad_v_heads, grad_cum_query, grad_cum_key = lax.map(
        backward_head,
        (query_heads, key_heads, value_heads, sent_cum, gathered_cum, log_total, grad_attn_heads),
    )
    grad_k_all = grad_k_heads.transpose(1, 0, 2).reshape(key_rows, width)
    grad_v_all = grad_v_heads.transpose(1, 0, 2).reshape(key_rows, width)
    grad_keys, grad_values, grad_key_cum = (
        lax.psum_scatter(grad_k_all, "ctx", scatter_dimension=0, tiled=True),
        lax.psum_scatter(grad_v_all, "ctx", scatter_dimension=0, tiled=True),
        lax.psum_scatter(grad_cum_key, "ctx", scatter_dimension=1, tiled=True),
    )
    grad_cum = grad_key_cum + grad_cum_query
    later_terms = prefix_2(
        jnp.sum(grad_cum, axis=1), "ctx", add_terms, jnp.zeros((heads,), jnp.float32), True
    )
    grad_cum = grad_cum + later_terms[:, None] * last_flag
    grad_log = lax.cumsum(grad_cum, axis=1, reverse=True).T
    grad_gate_pre = grad_log * jax.nn.sigmoid(-gate_pre)
    grad_forget_bias = jnp.sum(grad_gate_pre, axis=0)
    forget_low = grad_gate_pre.astype(jnp.bfloat16)
    grad_qn = grad_q.transpose(1, 0, 2)
    grad_kn = grad_keys.reshape(rows, heads, head_dim)
    grad_query_gain = jnp.sum(grad_qn * query * query_factor, axis=(0, 1))
    grad_key_gain = jnp.sum(grad_kn * keys * key_factor, axis=(0, 1))
    grad_query_raw = rms_back(query, query_factor, grad_qn, query_gain).reshape(rows, width)
    grad_key_raw = rms_back(keys, key_factor, grad_kn, key_gain).reshape(rows, width)
    qkv_low = jnp.concatenate([grad_query_raw, grad_key_raw, grad_values], axis=1).astype(
        jnp.bfloat16
    )
    grad_qkv = inner_rows(act_one, qkv_low)
    grad_forget = inner_rows(act_one, forget_low)
    grad_ogate = inner_rows(act_one, ogate_low)
    grad_act_one = (
        times_trans(qkv_low, qkv_back)
        + times_trans(forget_low, forget_back)
        + times_trans(ogate_low, ogate_back)
    )
    grad_norm_attn = jnp.sum(grad_act_one * inputs * factor_one, axis=0)
    grad_inputs = grad_middle + rms_back(inputs, factor_one, grad_act_one, norm_attn)
    summed = tuple(
        reduce_rows(piece)
        for piece in (grad_qkv, grad_forget, grad_ogate, grad_out, grad_gu, grad_down)
    )
    small = lax.psum(
        (
            grad_norm_attn,
            grad_norm_ffn,
            grad_query_gain,
            grad_key_gain,
            grad_forget_bias,
            grad_ogate_bias,
        ),
        ("dp", "fsdp", "ctx"),
    )
    return (
        result[None],
        grad_inputs[None],
        summed[0],
        summed[1],
        summed[2],
        summed[3],
        summed[4],
        summed[5],
        small[0],
        small[1],
        small[2],
        small[3],
        small[4],
        small[5],
    )


def solution(mesh):
    placed = (
        P(("dp", "fsdp"), "ctx", None),
        P(("dp", "fsdp"), "ctx", None),
        P("fsdp", None),
        P("fsdp", None),
        P("fsdp", None),
        P("fsdp", None),
        P("fsdp", None),
        P("fsdp", None),
        P(),
        P(),
        P(),
        P(),
        P(),
        P(),
    )
    return jax.shard_map(
        shards,
        mesh=mesh,
        in_specs=placed,
        out_specs=(
            P(("dp", "fsdp"), "ctx", None),
            P(("dp", "fsdp"), "ctx", None),
            P("fsdp", None),
            P("fsdp", None),
            P("fsdp", None),
            P("fsdp", None),
            P("fsdp", None),
            P("fsdp", None),
            P(),
            P(),
            P(),
            P(),
            P(),
            P(),
        ),
        check_vma=False,
    )
```

```python
import functools

import jax
import jax.numpy as jnp
from jax import lax
from jax.experimental import pallas as pl
from jax.experimental.pallas import tpu as pltpu
from jax.sharding import PartitionSpec as P

EPS = 1e-06
NEG_FILL = -1e30
LANES = 128
HALF = 64
TABLE = 16


def rms_factor(values):
    return lax.rsqrt(jnp.mean(values * values, axis=-1, keepdims=True) + EPS)


def rms_back(values, factor, grad_normed, gain):
    scaled = grad_normed * gain
    inner = jnp.mean(scaled * values, axis=-1, keepdims=True)
    return factor * scaled - factor * factor * factor * values * inner


def inner_rows(left, right):
    return lax.dot_general(
        left, right, (((0,), (0,)), ((), ())), preferred_element_type=jnp.float32
    )


def times_trans(left, right):
    return lax.dot_general(
        left, right, (((1,), (1,)), ((), ())), preferred_element_type=jnp.float32
    )


def lane_ids(rows):
    return lax.broadcasted_iota(jnp.int32, (rows, LANES), 1)


def head_half(pair_block, half):
    lanes = lane_ids(pair_block.shape[0])
    inside = (lanes < HALF) if half == 0 else (lanes >= HALF)
    return jnp.where(inside, pair_block, jnp.zeros_like(pair_block))


def both_halves(low, high):
    return jnp.where(lane_ids(low.shape[0]) < HALF, low, high)


def half_sums(values):
    lanes = lane_ids(values.shape[0])
    low = jnp.sum(jnp.where(lanes < HALF, values, 0.0), axis=1, keepdims=True)
    high = jnp.sum(jnp.where(lanes >= HALF, values, 0.0), axis=1, keepdims=True)
    return jnp.where(lanes < HALF, low, high)


def head_column(table, head):
    return jnp.sum(jnp.where(lane_ids(table.shape[0]) == head, table, 0.0), axis=1, keepdims=True)


def running_sum(values, reverse):
    rows = values.shape[0]
    at = lax.broadcasted_iota(jnp.int32, values.shape, 0)
    step = 1
    while step < rows:
        if reverse:
            moved = pltpu.roll(values, rows - step, 0)
            values = values + jnp.where(at < rows - step, moved, 0.0)
        else:
            moved = pltpu.roll(values, step, 0)
            values = values + jnp.where(at >= step, moved, 0.0)
        step *= 2
    return values


def log_sigmoid(values):
    return jnp.minimum(values, 0.0) - jnp.log(1.0 + jnp.exp(-jnp.abs(values)))


def prep_kernel(q_ref, k_ref, v_ref, f_ref, gq_ref, gk_ref, bias_ref, qn_ref, kn_ref, vb_ref, cum_ref, cumt_ref):
    query = q_ref[...]
    factor = lax.rsqrt(half_sums(query * query) * (1.0 / HALF) + EPS)
    low = (query * factor * gq_ref[...]).astype(jnp.bfloat16)
    qn_ref[...] = (low.astype(jnp.float32) * HALF ** (-0.5)).astype(jnp.bfloat16)
    keys = k_ref[...]
    factor = lax.rsqrt(half_sums(keys * keys) * (1.0 / HALF) + EPS)
    kn_ref[...] = (keys * factor * gk_ref[...]).astype(jnp.bfloat16)
    vb_ref[...] = v_ref[...].astype(jnp.bfloat16)

    @pl.when(pl.program_id(0) == 0)
    def _():
        cum = running_sum(log_sigmoid(f_ref[...] + bias_ref[...]), False)
        cum_ref[...] = cum
        cumt_ref[...] = cum.T[: cumt_ref.shape[0]]


def weigh(q_half, k_block, row_term, col_term, masked):
    scores = times_trans(q_half, k_block) + row_term - col_term
    if masked:
        rows = lax.broadcasted_iota(jnp.int32, scores.shape, 0)
        cols = lax.broadcasted_iota(jnp.int32, scores.shape, 1)
        scores = jnp.where(cols <= rows, scores, NEG_FILL)
    return jnp.exp(scores)


def forward_kernel(q_ref, k_ref, v_ref, kp_ref, vp_ref, cum_ref, cumt_ref, cumtp_ref, o_ref, rowc_ref, acc, tot):
    pair = pl.program_id(0)
    rows = q_ref.shape[0]
    block = rows // 2
    past = lax.axis_index("ctx") > 0

    @pl.when(pair == 0)
    def _():
        rowc_ref[...] = jnp.zeros_like(rowc_ref)

    for half in range(2):
        head = 2 * pair + half
        col = cumt_ref[pl.ds(head, 1), :]
        for qb in range(2):
            span = slice(qb * block, (qb + 1) * block)
            row = head_column(cum_ref[span, :], head)
            q_half = head_half(q_ref[span, :], half)
            weights = weigh(q_half, k_ref[span, :], row, col[:, span], True)
            total = jnp.sum(weights, axis=1, keepdims=True)
            attended = jnp.dot(
                weights.astype(jnp.bfloat16), v_ref[span, :], preferred_element_type=jnp.float32
            )
            if qb == 1:
                weights = weigh(q_half, k_ref[:block, :], row, col[:, :block], False)
                total = total + jnp.sum(weights, axis=1, keepdims=True)
                attended = attended + jnp.dot(
                    weights.astype(jnp.bfloat16), v_ref[:block, :], preferred_element_type=jnp.float32
                )
            acc[half, span, :] = attended
            tot[half, span, :] = total

    @pl.when(past)
    def _():
        for half in range(2):
            head = 2 * pair + half
            col = cumtp_ref[pl.ds(head, 1), :]
            col = col - col[:, rows - 1 : rows]
            for qb in range(2):
                span = slice(qb * block, (qb + 1) * block)
                row = head_column(cum_ref[span, :], head)
                q_half = head_half(q_ref[span, :], half)
                weights = weigh(q_half, kp_ref[...], row, col, False)
                acc[half, span, :] += jnp.dot(
                    weights.astype(jnp.bfloat16), vp_ref[...], preferred_element_type=jnp.float32
                )
                tot[half, span, :] += jnp.sum(weights, axis=1, keepdims=True)

    o_ref[...] = both_halves(acc[0] / tot[0], acc[1] / tot[1])
    lanes = lane_ids(rows)
    table = rowc_ref[...]
    for half in range(2):
        head = 2 * pair + half
        row = head_column(cum_ref[...], head) - jnp.log(tot[half])
        table = jnp.where(lanes == head, row, table)
    rowc_ref[...] = table


def backward_kernel(
    q_ref, k_ref, v_ref, kp_ref, vp_ref, do_ref, rowc_ref, cumt_ref, cumtp_ref,
    dq_ref, dk_ref, dv_ref, dkp_ref, dvp_ref, dcq_ref, dck_ref, dckp_ref, kacc, vacc,
):
    pair = pl.program_id(0)
    rows = q_ref.shape[0]
    block = rows // 2
    rank = lax.axis_index("ctx")

    @pl.when(pair == 0)
    def _():
        dcq_ref[...] = jnp.zeros_like(dcq_ref)
        dck_ref[...] = jnp.zeros_like(dck_ref)
        dckp_ref[...] = jnp.zeros_like(dckp_ref)

    def run(with_past):
        kacc[...] = jnp.zeros_like(kacc)
        vacc[...] = jnp.zeros_like(vacc)
        for half in range(2):
            head = 2 * pair + half
            col = cumt_ref[pl.ds(head, 1), :]
            if with_past:
                colp = cumtp_ref[pl.ds(head, 1), :]
                colp = colp - colp[:, rows - 1 : rows]
            down_total = jnp.zeros((1, 1), jnp.float32)
            for qb in range(2):
                span = slice(qb * block, (qb + 1) * block)
                row = head_column(rowc_ref[span, :], head)
                q_half = head_half(q_ref[span, :], half)
                do_half = head_half(do_ref[span, :], half)
                pieces = [(k_ref, v_ref, span, col[:, span], True, 0)]
                if qb == 1:
                    pieces.append((k_ref, v_ref, slice(0, block), col[:, :block], False, 0))
                if with_past:
                    for kb in range(2):
                        part = slice(kb * block, (kb + 1) * block)
                        pieces.append((kp_ref, vp_ref, part, colp[:, part], False, 1))
                probs, grads = [], []
                delta = jnp.zeros((block, 1), jnp.float32)
                for keys, values, part, cols, masked, where in pieces:
                    prob = weigh(q_half, keys[part, :], row, cols, masked)
                    grad = times_trans(do_half, values[part, :])
                    delta = delta + jnp.sum(prob * grad, axis=1, keepdims=True)
                    vacc[where, part, :] += inner_rows(prob.astype(jnp.bfloat16), do_half)
                    probs.append(prob)
                    grads.append(grad)
                query_grad = jnp.zeros((block, LANES), jnp.float32)
                row_sum = jnp.zeros((block, 1), jnp.float32)
                for (keys, values, part, cols, masked, where), prob, grad in zip(pieces, probs, grads):
                    score_grad = prob * (grad - delta)
                    low = score_grad.astype(jnp.bfloat16)
                    query_grad = query_grad + jnp.dot(
                        low, keys[part, :], preferred_element_type=jnp.float32
                    )
                    kacc[where, part, :] += inner_rows(low, q_half)
                    row_sum = row_sum + jnp.sum(score_grad, axis=1, keepdims=True)
                    col_sum = jnp.sum(score_grad, axis=0, keepdims=True)
                    target = dckp_ref if where else dck_ref
                    target[pl.ds(head, 1), part] += -col_sum
                    if not where:
                        down_total = down_total - jnp.sum(col_sum, axis=1, keepdims=True)
                query_grad = query_grad * HALF ** (-0.5)
                if half == 0:
                    dq_ref[span, :] = query_grad
                else:
                    dq_ref[span, :] = both_halves(dq_ref[span, :], query_grad)
                dcq_ref[span, :] = jnp.where(lane_ids(block) == head, row_sum, dcq_ref[span, :])
                down_total = down_total + jnp.sum(row_sum, axis=0, keepdims=True)
            table = dckp_ref[:, rows:]
            at = lax.broadcasted_iota(jnp.int32, table.shape, 0)
            dckp_ref[:, rows:] = jnp.where(at == head, down_total, table)
        dk_ref[...] = kacc[0]
        dv_ref[...] = vacc[0]
        dkp_ref[...] = kacc[1].astype(jnp.bfloat16)
        dvp_ref[...] = vacc[1].astype(jnp.bfloat16)

    @pl.when(rank == 0)
    def _():
        run(False)

    @pl.when(rank > 0)
    def _():
        run(True)


def rms_back_pair(values, grad, gain):
    factor = lax.rsqrt(half_sums(values * values) * (1.0 / HALF) + EPS)
    scaled = grad * gain
    inner = half_sums(scaled * values) * (1.0 / HALF)
    gain_grad = jnp.sum(grad * values * factor, axis=0, keepdims=True)
    return factor * scaled - factor * factor * factor * values * inner, gain_grad


def post_kernel(
    q_ref, k_ref, f_ref, gq_ref, gk_ref, bias_ref, dq_ref, dk_ref, dv_ref, dkr_ref, dvr_ref,
    dcq_ref, dck_ref, dckr_ref, dog_ref, out_ref, gains_ref, dbias_ref, flip,
):
    pair = pl.program_id(0)
    pairs = pl.num_programs(0)
    rows = q_ref.shape[0]
    width = pairs * LANES

    def place(base):
        return pl.ds(pl.multiple_of(base + pair * LANES, LANES), LANES)

    grad, query_gain = rms_back_pair(q_ref[...], dq_ref[...], gq_ref[...])
    out_ref[:, place(0)] = grad.astype(jnp.bfloat16)
    key_grad = dk_ref[...] + dkr_ref[...].astype(jnp.float32)
    grad, key_gain = rms_back_pair(k_ref[...], key_grad, gk_ref[...])
    out_ref[:, place(width)] = grad.astype(jnp.bfloat16)
    out_ref[:, place(2 * width)] = (dv_ref[...] + dvr_ref[...].astype(jnp.float32)).astype(jnp.bfloat16)
    out_ref[:, place(3 * width)] = dog_ref[...]

    @pl.when(pair == 0)
    def _():
        gains_ref[...] = jnp.zeros_like(gains_ref)
        count = dck_ref.shape[0]
        flip[...] = jnp.zeros_like(flip)
        flip[:count, :] = dck_ref[...] + dckr_ref[:, :rows]
        cum_grad = dcq_ref[...] + flip[...].T
        flip[...] = jnp.zeros_like(flip)
        flip[:count, :LANES] = dckr_ref[:, rows:]
        later = flip[:, :LANES].T[:1, :]
        log_grad = running_sum(cum_grad, True) + later
        gate = f_ref[...] + bias_ref[...]
        gate_grad = log_grad * jax.nn.sigmoid(-gate)
        dbias_ref[...] = jnp.broadcast_to(jnp.sum(gate_grad, axis=0, keepdims=True), dbias_ref.shape)
        out_ref[:, 4 * width :] = gate_grad.astype(jnp.bfloat16)

    gains_ref[0:1, :] += query_gain
    gains_ref[1:2, :] += key_gain


def gather_weights(mesh, pieces):
    groups, levels, halves = mesh.shape["dp"] * mesh.shape["ctx"], mesh.shape["fsdp"], mesh.shape["ctx"]
    count = len(pieces)
    chips = groups // 2

    def body(*refs):
        ins, outs = refs[:count], refs[count : 2 * count]
        keep_sem, z_sem, peer_sem, core_sem, got_sem = refs[2 * count :]
        dp, z, y = lax.axis_index("dp"), lax.axis_index("fsdp"), lax.axis_index("ctx")
        core = dp % 2
        mine = dp * halves + y
        chip = (dp // 2) * halves + y

        def group_of(other_chip, other_core):
            return ((other_chip // halves) * 2 + other_core) * halves + other_chip % halves

        def place(group, level):
            return {"dp": group // halves, "fsdp": level, "ctx": group % halves}

        barrier = pltpu.get_barrier_semaphore()

        def greet(group, level):
            pl.semaphore_signal(
                barrier, inc=1, device_id=place(group, level), device_id_type=pl.DeviceIdType.MESH
            )

        sibling = group_of(chip, 1 - core)
        greet(sibling, z)
        for hop in range(1, chips):
            greet(group_of((chip + hop) % chips, core), z)

        @pl.when(z > 0)
        def _():
            greet(mine, z - 1)

        @pl.when(z < levels - 1)
        def _():
            greet(mine, z + 1)

        ends = jnp.minimum(z, 1) + jnp.minimum(levels - 1 - z, 1)
        pl.semaphore_wait(barrier, chips + ends)

        def copy(a, level, group, to_group, to_level, sem, own=False):
            slot = level * groups + group
            return pltpu.make_async_remote_copy(
                src_ref=ins[a].at[group] if own else outs[a].at[slot],
                dst_ref=outs[a].at[slot],
                send_sem=sem,
                recv_sem=got_sem.at[a, slot],
                device_id=place(to_group, to_level),
                device_id_type=pl.DeviceIdType.MESH,
            )

        def z_copy(a, level, side, own=False):
            return copy(a, level, mine, mine, z + (1 if side else -1), z_sem.at[a, level, side], own)

        def peer_copy(a, level, hop):
            return copy(a, level, mine, group_of((chip + hop) % chips, core), z, peer_sem.at[a, level, hop])

        def core_copy(a, level, hop):
            return copy(a, level, group_of((chip + hop) % chips, core), sibling, z, core_sem.at[a, level, hop])

        def arrived(a, level, group):
            copy(a, level, group, sibling, z, core_sem.at[a, level, 0]).wait_recv()

        def kept(a):
            return pltpu.make_async_copy(ins[a], outs[a].at[pl.ds(z * groups, groups)], keep_sem.at[a])

        def edges(action):
            for a in range(count):

                @pl.when(z < levels - 1)
                def _():
                    action(z_copy(a, z, 1, True))

                @pl.when(z > 0)
                def _():
                    action(z_copy(a, z, 0, True))

        edges(lambda item: item.start())
        for a in range(count):
            kept(a).start()

        def near(a, level, side, last):
            arrived(a, level, mine)

            @pl.when(jnp.logical_not(last))
            def _():
                z_copy(a, level, side).start()

            for hop in range(1, chips):
                peer_copy(a, level, hop).start()
            core_copy(a, level, 0).start()

        for a in range(count):
            for step in range(1, levels):

                @pl.when(z - step >= 0)
                def _():
                    near(a, z - step, 1, z == levels - 1)

                @pl.when(z + step < levels)
                def _():
                    near(a, z + step, 0, z == 0)

        def others(action):
            for a in range(count):
                for step in range(1, levels):
                    level = (z + step) % levels
                    action(a, level)

        def spread(a, level):
            for hop in range(1, chips):
                arrived(a, level, group_of((chip + hop) % chips, core))
                core_copy(a, level, hop).start()

        def finish(a, level):
            for hop in range(chips):
                arrived(a, level, group_of((chip + hop) % chips, 1 - core))
            for hop in range(chips):
                core_copy(a, level, hop).wait_send()
            for hop in range(1, chips):
                peer_copy(a, level, hop).wait_send()

        others(spread)
        others(finish)
        edges(lambda item: item.wait_send())
        for a in range(count):
            kept(a).wait()
            for step in range(1, levels):

                @pl.when(jnp.logical_and(z - step >= 0, z < levels - 1))
                def _():
                    z_copy(a, z - step, 1).wait_send()

                @pl.when(jnp.logical_and(z + step < levels, z > 0))
                def _():
                    z_copy(a, z + step, 0).wait_send()

    dma = pltpu.SemaphoreType.DMA
    return pl.pallas_call(
        body,
        out_shape=[
            jax.ShapeDtypeStruct((levels * groups,) + piece.shape[1:], piece.dtype) for piece in pieces
        ],
        in_specs=[pl.BlockSpec(memory_space=pltpu.VMEM)] * count,
        out_specs=[pl.BlockSpec(memory_space=pl.ANY)] * count,
        scratch_shapes=[
            dma((count,)),
            dma((count, levels, 2)),
            dma((count, levels, chips)),
            dma((count, levels, chips)),
            dma((count, levels * groups)),
        ],
        compiler_params=pltpu.CompilerParams(collective_id=1, has_side_effects=True),
        name="gather_weights",
    )(*pieces)


def reduce_all(mesh, grads, small):
    axes = ("fsdp", "dp", "ctx")
    pieces = mesh.shape["fsdp"] * mesh.shape["dp"] * mesh.shape["ctx"]
    flat = jnp.concatenate(
        [grad.astype(jnp.bfloat16).reshape(pieces, -1) for grad in grads], axis=1
    ).reshape(-1, LANES)
    part = lax.psum_scatter(flat, axes, scatter_dimension=0, tiled=True)
    level = lax.all_gather(part, ("dp", "ctx"), axis=0, tiled=True).astype(jnp.float32)
    level = level.reshape(pieces // mesh.shape["fsdp"], -1)
    owned, start = [], 0
    for grad in grads:
        size = grad.size // pieces
        rows = grad.shape[0] // mesh.shape["fsdp"]
        owned.append(level[:, start : start + size].reshape(rows, grad.shape[1]))
        start += size
    total = lax.psum(jnp.concatenate(small), axes)
    sums, start = [], 0
    for part in small:
        sums.append(total[start : start + part.shape[0]])
        start += part.shape[0]
    return owned, sums


def prepare(proj, gains, bias, pairs):
    rows = proj.shape[0]
    col = lambda base: pl.BlockSpec((rows, LANES), lambda p: (0, base + p))
    fixed = lambda shape: pl.BlockSpec(shape, lambda p: (0, 0))
    low = jax.ShapeDtypeStruct((rows, pairs * LANES), jnp.bfloat16)
    return pl.pallas_call(
        prep_kernel,
        grid=(pairs,),
        out_shape=[
            low, low, low,
            jax.ShapeDtypeStruct((rows, LANES), jnp.float32),
            jax.ShapeDtypeStruct((TABLE, rows), jnp.float32),
        ],
        in_specs=[
            col(0), col(pairs), col(2 * pairs),
            pl.BlockSpec((rows, LANES), lambda p: (0, 4 * pairs)),
            fixed((1, LANES)), fixed((1, LANES)), fixed((1, LANES)),
        ],
        out_specs=[col(0), col(0), col(0), fixed((rows, LANES)), fixed((TABLE, rows))],
        name="prep",
    )(proj, proj, proj, proj, gains[0], gains[1], bias)


def attend(qn, kn, vb, kp, vp, cum, cumt, cumtp, pairs):
    rows = qn.shape[0]
    col = pl.BlockSpec((rows, LANES), lambda p: (0, p))
    fixed = lambda shape: pl.BlockSpec(shape, lambda p: (0, 0))
    return pl.pallas_call(
        forward_kernel,
        grid=(pairs,),
        out_shape=[
            jax.ShapeDtypeStruct((rows, pairs * LANES), jnp.float32),
            jax.ShapeDtypeStruct((rows, LANES), jnp.float32),
        ],
        in_specs=[col] * 5 + [fixed((rows, LANES)), fixed((TABLE, rows)), fixed((TABLE, rows))],
        out_specs=[col, fixed((rows, LANES))],
        scratch_shapes=[
            pltpu.VMEM((2, rows, LANES), jnp.float32),
            pltpu.VMEM((2, rows, 1), jnp.float32),
        ],
        name="attend",
    )(qn, kn, vb, kp, vp, cum, cumt, cumtp)


def attend_back(qn, kn, vb, kp, vp, grad, rowc, cumt, cumtp, pairs):
    rows = qn.shape[0]
    col = pl.BlockSpec((rows, LANES), lambda p: (0, p))
    fixed = lambda shape: pl.BlockSpec(shape, lambda p: (0, 0))
    wide = jax.ShapeDtypeStruct((rows, pairs * LANES), jnp.float32)
    low = jax.ShapeDtypeStruct((rows, pairs * LANES), jnp.bfloat16)
    shapes = [(rows, LANES), (TABLE, rows), (TABLE, rows + LANES)]
    return pl.pallas_call(
        backward_kernel,
        grid=(pairs,),
        out_shape=[wide, wide, wide, low, low]
        + [jax.ShapeDtypeStruct(shape, jnp.float32) for shape in shapes],
        in_specs=[col] * 6 + [fixed((rows, LANES)), fixed((TABLE, rows)), fixed((TABLE, rows))],
        out_specs=[col] * 5 + [fixed(shape) for shape in shapes],
        scratch_shapes=[pltpu.VMEM((2, rows, LANES), jnp.float32)] * 2,
        name="attend_back",
    )(qn, kn, vb, kp, vp, grad, rowc, cumt, cumtp)


def finish_back(proj, gains, bias, dq, dk, dv, dkr, dvr, dcq, dck, dckr, dog, pairs):
    rows = proj.shape[0]
    at = lambda base: pl.BlockSpec((rows, LANES), lambda p: (0, base + p))
    col = at(0)
    fixed = lambda shape: pl.BlockSpec(shape, lambda p: (0, 0))
    total = (4 * pairs + 1) * LANES
    return pl.pallas_call(
        post_kernel,
        grid=(pairs,),
        out_shape=[
            jax.ShapeDtypeStruct((rows, total), jnp.bfloat16),
            jax.ShapeDtypeStruct((8, LANES), jnp.float32),
            jax.ShapeDtypeStruct((8, LANES), jnp.float32),
        ],
        in_specs=[
            at(0), at(pairs), pl.BlockSpec((rows, LANES), lambda p: (0, 4 * pairs)),
            fixed((1, LANES)), fixed((1, LANES)), fixed((1, LANES)),
            col, col, col, col, col,
            fixed((rows, LANES)), fixed((TABLE, rows)), fixed((TABLE, rows + LANES)), col,
        ],
        out_specs=[fixed((rows, total)), fixed((8, LANES)), fixed((8, LANES))],
        scratch_shapes=[pltpu.VMEM((LANES, rows), jnp.float32)],
        name="finish_back",
    )(proj, proj, proj, gains[0], gains[1], bias, dq, dk, dv, dkr, dvr, dcq, dck, dckr, dog)


def shards(
    mesh,
    tokens,
    cotangent,
    w_qkv,
    w_forget,
    w_ogate,
    w_out,
    w_gu,
    w_down,
    norm_attn,
    norm_ffn,
    query_gain,
    key_gain,
    forget_bias,
    ogate_bias,
):
    inputs = tokens[0].astype(jnp.float32)
    grad_top = cotangent[0].astype(jnp.float32)
    grad_low = cotangent[0]
    rows, width = inputs.shape
    heads = forget_bias.shape[0]
    pairs = width // LANES
    hidden = w_gu.shape[1] // 2
    groups = mesh.shape["dp"] * mesh.shape["ctx"]
    levels = mesh.shape["fsdp"]
    cut = lambda shard: shard.reshape(groups, shard.shape[0] // groups, shard.shape[1])
    forget_wide = jnp.pad(w_forget, ((0, 0), (0, LANES - heads)))
    first = cut(jnp.concatenate([w_qkv, w_ogate, forget_wide], axis=1))
    second = cut(jnp.concatenate([w_out, w_gu], axis=1))
    proj_full, mid_full, down_full = (
        full.reshape(-1, full.shape[2]) for full in gather_weights(mesh, (first, second, cut(w_down)))
    )
    out_full, gu_full = mid_full[:, :width], mid_full[:, width:]

    factor_one = rms_factor(inputs)
    act_one = (inputs * factor_one * norm_attn).astype(jnp.bfloat16)
    proj = jnp.dot(act_one, proj_full, preferred_element_type=jnp.float32)
    gains = tuple(jnp.concatenate([gain, gain])[None] for gain in (query_gain, key_gain))
    bias = jnp.pad(forget_bias, (0, LANES - heads))[None]
    qn, kn, vb, cum, cumt = prepare(proj, gains, bias, pairs)
    kp, vp, cumtp = (lax.ppermute(part, "ctx", [(0, 1)]) for part in (kn, vb, cumt))
    attn, rowc = attend(qn, kn, vb, kp, vp, cum, cumt, cumtp, pairs)
    ogate = jax.nn.sigmoid(proj[:, 3 * width : 4 * width] + ogate_bias)
    gated = (attn * ogate).astype(jnp.bfloat16)
    middle = inputs + jnp.dot(gated, out_full, preferred_element_type=jnp.float32)
    factor_two = rms_factor(middle)
    act_two = (middle * factor_two * norm_ffn).astype(jnp.bfloat16)
    gate_up = jnp.dot(act_two, gu_full, preferred_element_type=jnp.float32)
    gate_part = gate_up[:, :hidden]
    up_part = gate_up[:, hidden:]
    hidden_low = (jax.nn.silu(gate_part) * up_part).astype(jnp.bfloat16)
    result = middle + jnp.dot(hidden_low, down_full, preferred_element_type=jnp.float32)

    grad_down = inner_rows(hidden_low, grad_low)
    grad_hidden = times_trans(grad_low, down_full)
    sigma = jax.nn.sigmoid(gate_part)
    grad_gu_low = jnp.concatenate(
        [
            grad_hidden * up_part * sigma * (1.0 + gate_part * (1.0 - sigma)),
            grad_hidden * (gate_part * sigma),
        ],
        axis=1,
    ).astype(jnp.bfloat16)
    grad_gu = inner_rows(act_two, grad_gu_low)
    grad_act_two = times_trans(grad_gu_low, gu_full)
    grad_norm_ffn = jnp.sum(grad_act_two * middle * factor_two, axis=0)
    grad_middle = grad_top + rms_back(middle, factor_two, grad_act_two, norm_ffn)
    middle_low = grad_middle.astype(jnp.bfloat16)
    grad_out = inner_rows(gated, middle_low)
    grad_gated = times_trans(middle_low, out_full)
    grad_attn_low = (grad_gated * ogate).astype(jnp.bfloat16)
    grad_ogate_pre = grad_gated * attn * ogate * (1.0 - ogate)
    grad_ogate_bias = jnp.sum(grad_ogate_pre, axis=0)
    ogate_low = grad_ogate_pre.astype(jnp.bfloat16)

    dq, dk, dv, dkp, dvp, dcq, dck, dckp = attend_back(
        qn, kn, vb, kp, vp, grad_attn_low, rowc, cumt, cumtp, pairs
    )
    dkr, dvr, dckr = (lax.ppermute(part, "ctx", [(1, 0)]) for part in (dkp, dvp, dckp))
    proj_low, gain_sums, bias_sums = finish_back(
        proj, gains, bias, dq, dk, dv, dkr, dvr, dcq, dck, dckr, ogate_low, pairs
    )
    grad_proj = inner_rows(act_one, proj_low)
    grad_act_one = times_trans(proj_low, proj_full)
    grad_norm_attn = jnp.sum(grad_act_one * inputs * factor_one, axis=0)
    grad_inputs = grad_middle + rms_back(inputs, factor_one, grad_act_one, norm_attn)

    small = (
        grad_norm_attn,
        grad_norm_ffn,
        gain_sums[0, :HALF] + gain_sums[0, HALF:],
        gain_sums[1, :HALF] + gain_sums[1, HALF:],
        bias_sums[0, :heads],
        grad_ogate_bias,
    )
    owned, small = reduce_all(mesh, (grad_proj, grad_out, grad_gu, grad_down), small)
    own_proj, own_out, own_gu, own_down = owned
    return (
        result[None],
        grad_inputs[None],
        own_proj[:, : 3 * width],
        own_proj[:, 4 * width : 4 * width + heads],
        own_proj[:, 3 * width : 4 * width],
        own_out,
        own_gu,
        own_down,
    ) + tuple(small)


def solution(mesh):
    block = P(("dp", "fsdp"), "ctx", None)
    rows = P("fsdp", None)
    return jax.shard_map(
        functools.partial(shards, mesh),
        mesh=mesh,
        in_specs=(block, block) + (rows,) * 6 + (P(),) * 6,
        out_specs=(block, block) + (rows,) * 6 + (P(),) * 6,
        check_vma=False,
    )
```

```python
import functools

import jax
import jax.numpy as jnp
from jax import lax
from jax.experimental import pallas as pl
from jax.experimental.pallas import tpu as pltpu
from jax.sharding import PartitionSpec as P

EPS = 1e-06
NEG_FILL = -1e30
LANES = 128
HALF = 64
TABLE = 16


def rms_factor(values):
    return lax.rsqrt(jnp.mean(values * values, axis=-1, keepdims=True) + EPS)


def rms_back(values, factor, grad_normed, gain):
    scaled = grad_normed * gain
    inner = jnp.mean(scaled * values, axis=-1, keepdims=True)
    return factor * scaled - factor * factor * factor * values * inner


def inner_rows(left, right):
    return lax.dot_general(
        left, right, (((0,), (0,)), ((), ())), preferred_element_type=jnp.float32
    )


def times_trans(left, right):
    return lax.dot_general(
        left, right, (((1,), (1,)), ((), ())), preferred_element_type=jnp.float32
    )


def lane_ids(rows):
    return lax.broadcasted_iota(jnp.int32, (rows, LANES), 1)


def head_half(pair_block, half):
    lanes = lane_ids(pair_block.shape[0])
    inside = (lanes < HALF) if half == 0 else (lanes >= HALF)
    return jnp.where(inside, pair_block, jnp.zeros_like(pair_block))


def both_halves(low, high):
    return jnp.where(lane_ids(low.shape[0]) < HALF, low, high)


def half_sums(values):
    lanes = lane_ids(values.shape[0])
    low = jnp.sum(jnp.where(lanes < HALF, values, 0.0), axis=1, keepdims=True)
    high = jnp.sum(jnp.where(lanes >= HALF, values, 0.0), axis=1, keepdims=True)
    return jnp.where(lanes < HALF, low, high)


def head_column(table, head):
    return jnp.sum(jnp.where(lane_ids(table.shape[0]) == head, table, 0.0), axis=1, keepdims=True)


def running_sum(values, reverse):
    rows = values.shape[0]
    at = lax.broadcasted_iota(jnp.int32, values.shape, 0)
    step = 1
    while step < rows:
        if reverse:
            moved = pltpu.roll(values, rows - step, 0)
            values = values + jnp.where(at < rows - step, moved, 0.0)
        else:
            moved = pltpu.roll(values, step, 0)
            values = values + jnp.where(at >= step, moved, 0.0)
        step *= 2
    return values


def log_sigmoid(values):
    return jnp.minimum(values, 0.0) - jnp.log(1.0 + jnp.exp(-jnp.abs(values)))


def prep_kernel(q_ref, k_ref, v_ref, f_ref, gq_ref, gk_ref, bias_ref, qn_ref, kn_ref, vb_ref, cum_ref, cumt_ref):
    query = q_ref[...]
    factor = lax.rsqrt(half_sums(query * query) * (1.0 / HALF) + EPS)
    low = (query * factor * gq_ref[...]).astype(jnp.bfloat16)
    qn_ref[...] = (low.astype(jnp.float32) * HALF ** (-0.5)).astype(jnp.bfloat16)
    keys = k_ref[...]
    factor = lax.rsqrt(half_sums(keys * keys) * (1.0 / HALF) + EPS)
    kn_ref[...] = (keys * factor * gk_ref[...]).astype(jnp.bfloat16)
    vb_ref[...] = v_ref[...].astype(jnp.bfloat16)

    @pl.when(pl.program_id(0) == 0)
    def _():
        cum = running_sum(log_sigmoid(f_ref[...] + bias_ref[...]), False)
        cum_ref[...] = cum
        cumt_ref[...] = cum.T[: cumt_ref.shape[0]]


def weigh(q_half, k_block, row_term, col_term, masked):
    scores = times_trans(q_half, k_block) + row_term - col_term
    if masked:
        rows = lax.broadcasted_iota(jnp.int32, scores.shape, 0)
        cols = lax.broadcasted_iota(jnp.int32, scores.shape, 1)
        scores = jnp.where(cols <= rows, scores, NEG_FILL)
    return jnp.exp(scores)


def forward_kernel(q_ref, k_ref, v_ref, kp_ref, vp_ref, cum_ref, cumt_ref, cumtp_ref, o_ref, rowc_ref, acc, tot):
    pair = pl.program_id(0)
    rows = q_ref.shape[0]
    block = rows // 2
    past = lax.axis_index("ctx") > 0

    @pl.when(pair == 0)
    def _():
        rowc_ref[...] = jnp.zeros_like(rowc_ref)

    for half in range(2):
        head = 2 * pair + half
        col = cumt_ref[pl.ds(head, 1), :]
        for qb in range(2):
            span = slice(qb * block, (qb + 1) * block)
            row = head_column(cum_ref[span, :], head)
            q_half = head_half(q_ref[span, :], half)
            weights = weigh(q_half, k_ref[span, :], row, col[:, span], True)
            total = jnp.sum(weights, axis=1, keepdims=True)
            attended = jnp.dot(
                weights.astype(jnp.bfloat16), v_ref[span, :], preferred_element_type=jnp.float32
            )
            if qb == 1:
                weights = weigh(q_half, k_ref[:block, :], row, col[:, :block], False)
                total = total + jnp.sum(weights, axis=1, keepdims=True)
                attended = attended + jnp.dot(
                    weights.astype(jnp.bfloat16), v_ref[:block, :], preferred_element_type=jnp.float32
                )
            acc[half, span, :] = attended
            tot[half, span, :] = total

    @pl.when(past)
    def _():
        for half in range(2):
            head = 2 * pair + half
            col = cumtp_ref[pl.ds(head, 1), :]
            col = col - col[:, rows - 1 : rows]
            for qb in range(2):
                span = slice(qb * block, (qb + 1) * block)
                row = head_column(cum_ref[span, :], head)
                q_half = head_half(q_ref[span, :], half)
                weights = weigh(q_half, kp_ref[...], row, col, False)
                acc[half, span, :] += jnp.dot(
                    weights.astype(jnp.bfloat16), vp_ref[...], preferred_element_type=jnp.float32
                )
                tot[half, span, :] += jnp.sum(weights, axis=1, keepdims=True)

    o_ref[...] = both_halves(acc[0] / tot[0], acc[1] / tot[1])
    lanes = lane_ids(rows)
    table = rowc_ref[...]
    for half in range(2):
        head = 2 * pair + half
        row = head_column(cum_ref[...], head) - jnp.log(tot[half])
        table = jnp.where(lanes == head, row, table)
    rowc_ref[...] = table


def backward_kernel(
    q_ref, k_ref, v_ref, kp_ref, vp_ref, do_ref, rowc_ref, cumt_ref, cumtp_ref,
    dq_ref, dk_ref, dv_ref, dkp_ref, dvp_ref, dcq_ref, dck_ref, dckp_ref, kacc, vacc,
):
    pair = pl.program_id(0)
    rows = q_ref.shape[0]
    block = rows // 2
    rank = lax.axis_index("ctx")

    @pl.when(pair == 0)
    def _():
        dcq_ref[...] = jnp.zeros_like(dcq_ref)
        dck_ref[...] = jnp.zeros_like(dck_ref)
        dckp_ref[...] = jnp.zeros_like(dckp_ref)

    def run(with_past):
        kacc[...] = jnp.zeros_like(kacc)
        vacc[...] = jnp.zeros_like(vacc)
        for half in range(2):
            head = 2 * pair + half
            col = cumt_ref[pl.ds(head, 1), :]
            if with_past:
                colp = cumtp_ref[pl.ds(head, 1), :]
                colp = colp - colp[:, rows - 1 : rows]
            down_total = jnp.zeros((1, 1), jnp.float32)
            for qb in range(2):
                span = slice(qb * block, (qb + 1) * block)
                row = head_column(rowc_ref[span, :], head)
                q_half = head_half(q_ref[span, :], half)
                do_half = head_half(do_ref[span, :], half)
                pieces = [(k_ref, v_ref, span, col[:, span], True, 0)]
                if qb == 1:
                    pieces.append((k_ref, v_ref, slice(0, block), col[:, :block], False, 0))
                if with_past:
                    for kb in range(2):
                        part = slice(kb * block, (kb + 1) * block)
                        pieces.append((kp_ref, vp_ref, part, colp[:, part], False, 1))
                probs, grads = [], []
                delta = jnp.zeros((block, 1), jnp.float32)
                for keys, values, part, cols, masked, where in pieces:
                    prob = weigh(q_half, keys[part, :], row, cols, masked)
                    grad = times_trans(do_half, values[part, :])
                    delta = delta + jnp.sum(prob * grad, axis=1, keepdims=True)
                    vacc[where, part, :] += inner_rows(prob.astype(jnp.bfloat16), do_half)
                    probs.append(prob)
                    grads.append(grad)
                query_grad = jnp.zeros((block, LANES), jnp.float32)
                row_sum = jnp.zeros((block, 1), jnp.float32)
                for (keys, values, part, cols, masked, where), prob, grad in zip(pieces, probs, grads):
                    score_grad = prob * (grad - delta)
                    low = score_grad.astype(jnp.bfloat16)
                    query_grad = query_grad + jnp.dot(
                        low, keys[part, :], preferred_element_type=jnp.float32
                    )
                    kacc[where, part, :] += inner_rows(low, q_half)
                    row_sum = row_sum + jnp.sum(score_grad, axis=1, keepdims=True)
                    col_sum = jnp.sum(score_grad, axis=0, keepdims=True)
                    target = dckp_ref if where else dck_ref
                    target[pl.ds(head, 1), part] += -col_sum
                    if not where:
                        down_total = down_total - jnp.sum(col_sum, axis=1, keepdims=True)
                query_grad = query_grad * HALF ** (-0.5)
                if half == 0:
                    dq_ref[span, :] = query_grad
                else:
                    dq_ref[span, :] = both_halves(dq_ref[span, :], query_grad)
                dcq_ref[span, :] = jnp.where(lane_ids(block) == head, row_sum, dcq_ref[span, :])
                down_total = down_total + jnp.sum(row_sum, axis=0, keepdims=True)
            table = dckp_ref[:, rows:]
            at = lax.broadcasted_iota(jnp.int32, table.shape, 0)
            dckp_ref[:, rows:] = jnp.where(at == head, down_total, table)
        dk_ref[...] = kacc[0]
        dv_ref[...] = vacc[0]
        dkp_ref[...] = kacc[1].astype(jnp.bfloat16)
        dvp_ref[...] = vacc[1].astype(jnp.bfloat16)

    @pl.when(rank == 0)
    def _():
        run(False)

    @pl.when(rank > 0)
    def _():
        run(True)


def rms_back_pair(values, grad, gain):
    factor = lax.rsqrt(half_sums(values * values) * (1.0 / HALF) + EPS)
    scaled = grad * gain
    inner = half_sums(scaled * values) * (1.0 / HALF)
    gain_grad = jnp.sum(grad * values * factor, axis=0, keepdims=True)
    return factor * scaled - factor * factor * factor * values * inner, gain_grad


def post_kernel(
    q_ref, k_ref, f_ref, gq_ref, gk_ref, bias_ref, dq_ref, dk_ref, dv_ref, dkr_ref, dvr_ref,
    dcq_ref, dck_ref, dckr_ref, dog_ref, out_ref, gains_ref, dbias_ref, flip,
):
    pair = pl.program_id(0)
    pairs = pl.num_programs(0)
    rows = q_ref.shape[0]
    width = pairs * LANES

    def place(base):
        return pl.ds(pl.multiple_of(base + pair * LANES, LANES), LANES)

    grad, query_gain = rms_back_pair(q_ref[...], dq_ref[...], gq_ref[...])
    out_ref[:, place(0)] = grad.astype(jnp.bfloat16)
    key_grad = dk_ref[...] + dkr_ref[...].astype(jnp.float32)
    grad, key_gain = rms_back_pair(k_ref[...], key_grad, gk_ref[...])
    out_ref[:, place(width)] = grad.astype(jnp.bfloat16)
    out_ref[:, place(2 * width)] = (dv_ref[...] + dvr_ref[...].astype(jnp.float32)).astype(jnp.bfloat16)
    out_ref[:, place(3 * width)] = dog_ref[...]

    @pl.when(pair == 0)
    def _():
        gains_ref[...] = jnp.zeros_like(gains_ref)
        count = dck_ref.shape[0]
        flip[...] = jnp.zeros_like(flip)
        flip[:count, :] = dck_ref[...] + dckr_ref[:, :rows]
        cum_grad = dcq_ref[...] + flip[...].T
        flip[...] = jnp.zeros_like(flip)
        flip[:count, :LANES] = dckr_ref[:, rows:]
        later = flip[:, :LANES].T[:1, :]
        log_grad = running_sum(cum_grad, True) + later
        gate = f_ref[...] + bias_ref[...]
        gate_grad = log_grad * jax.nn.sigmoid(-gate)
        dbias_ref[...] = jnp.broadcast_to(jnp.sum(gate_grad, axis=0, keepdims=True), dbias_ref.shape)
        out_ref[:, 4 * width :] = gate_grad.astype(jnp.bfloat16)

    gains_ref[0:1, :] += query_gain
    gains_ref[1:2, :] += key_gain


def gather_weights(mesh, pieces):
    groups, levels, halves = mesh.shape["dp"] * mesh.shape["ctx"], mesh.shape["fsdp"], mesh.shape["ctx"]
    count = len(pieces)
    chips = groups // 2

    def body(*refs):
        ins, outs = refs[:count], refs[count : 2 * count]
        keep_sem, z_sem, peer_sem, core_sem, got_sem = refs[2 * count :]
        dp, z, y = lax.axis_index("dp"), lax.axis_index("fsdp"), lax.axis_index("ctx")
        core = dp % 2
        mine = dp * halves + y
        chip = (dp // 2) * halves + y

        def group_of(other_chip, other_core):
            return ((other_chip // halves) * 2 + other_core) * halves + other_chip % halves

        def place(group, level):
            return {"dp": group // halves, "fsdp": level, "ctx": group % halves}

        barrier = pltpu.get_barrier_semaphore()

        def greet(group, level):
            pl.semaphore_signal(
                barrier, inc=1, device_id=place(group, level), device_id_type=pl.DeviceIdType.MESH
            )

        sibling = group_of(chip, 1 - core)
        greet(sibling, z)
        for hop in range(1, chips):
            greet(group_of((chip + hop) % chips, core), z)

        @pl.when(z > 0)
        def _():
            greet(mine, z - 1)

        @pl.when(z < levels - 1)
        def _():
            greet(mine, z + 1)

        ends = jnp.minimum(z, 1) + jnp.minimum(levels - 1 - z, 1)
        pl.semaphore_wait(barrier, chips + ends)

        def copy(a, level, group, to_group, to_level, sem, own=False):
            slot = level * groups + group
            return pltpu.make_async_remote_copy(
                src_ref=ins[a].at[group] if own else outs[a].at[slot],
                dst_ref=outs[a].at[slot],
                send_sem=sem,
                recv_sem=got_sem.at[a, slot],
                device_id=place(to_group, to_level),
                device_id_type=pl.DeviceIdType.MESH,
            )

        def z_copy(a, level, side, own=False):
            return copy(a, level, mine, mine, z + (1 if side else -1), z_sem.at[a, level, side], own)

        def peer_copy(a, level, hop):
            return copy(a, level, mine, group_of((chip + hop) % chips, core), z, peer_sem.at[a, level, hop])

        def core_copy(a, level, hop):
            return copy(a, level, group_of((chip + hop) % chips, core), sibling, z, core_sem.at[a, level, hop])

        def arrived(a, level, group):
            copy(a, level, group, sibling, z, core_sem.at[a, level, 0]).wait_recv()

        def kept(a):
            return pltpu.make_async_copy(ins[a], outs[a].at[pl.ds(z * groups, groups)], keep_sem.at[a])

        def edges(action):
            for a in range(count):

                @pl.when(z < levels - 1)
                def _():
                    action(z_copy(a, z, 1, True))

                @pl.when(z > 0)
                def _():
                    action(z_copy(a, z, 0, True))

        edges(lambda item: item.start())
        for a in range(count):
            kept(a).start()

        def near(a, level, side, last):
            arrived(a, level, mine)

            @pl.when(jnp.logical_not(last))
            def _():
                z_copy(a, level, side).start()

            for hop in range(1, chips):
                peer_copy(a, level, hop).start()
            core_copy(a, level, 0).start()

        for a in range(count):
            for step in range(1, levels):

                @pl.when(z - step >= 0)
                def _():
                    near(a, z - step, 1, z == levels - 1)

                @pl.when(z + step < levels)
                def _():
                    near(a, z + step, 0, z == 0)

        def others(action):
            for a in range(count):
                for step in range(1, levels):
                    level = (z + step) % levels
                    action(a, level)

        def spread(a, level):
            for hop in range(1, chips):
                arrived(a, level, group_of((chip + hop) % chips, core))
                core_copy(a, level, hop).start()

        def finish(a, level):
            for hop in range(chips):
                arrived(a, level, group_of((chip + hop) % chips, 1 - core))
            for hop in range(chips):
                core_copy(a, level, hop).wait_send()
            for hop in range(1, chips):
                peer_copy(a, level, hop).wait_send()

        others(spread)
        others(finish)
        edges(lambda item: item.wait_send())
        for a in range(count):
            kept(a).wait()
            for step in range(1, levels):

                @pl.when(jnp.logical_and(z - step >= 0, z < levels - 1))
                def _():
                    z_copy(a, z - step, 1).wait_send()

                @pl.when(jnp.logical_and(z + step < levels, z > 0))
                def _():
                    z_copy(a, z + step, 0).wait_send()

    dma = pltpu.SemaphoreType.DMA
    return pl.pallas_call(
        body,
        out_shape=[
            jax.ShapeDtypeStruct((levels * groups,) + piece.shape[1:], piece.dtype) for piece in pieces
        ],
        in_specs=[pl.BlockSpec(memory_space=pltpu.VMEM)] * count,
        out_specs=[pl.BlockSpec(memory_space=pl.ANY)] * count,
        scratch_shapes=[
            dma((count,)),
            dma((count, levels, 2)),
            dma((count, levels, chips)),
            dma((count, levels, chips)),
            dma((count, levels * groups)),
        ],
        compiler_params=pltpu.CompilerParams(collective_id=1, has_side_effects=True),
        name="gather_weights",
    )(*pieces)


def reduce_kernel(mesh, grads, small):
    halves, levels = mesh.shape["ctx"], mesh.shape["fsdp"]
    groups = mesh.shape["dp"] * halves
    chips = groups // 2
    count = len(grads)
    wide = jnp.float32

    def body(*refs):
        ins, small_in = refs[:count], refs[count]
        outs, small_out = refs[count + 1 : 2 * count + 1], refs[2 * count + 1]
        rest = refs[2 * count + 2 :]
        pair_buf, quad_buf, z_buf = rest[:count], rest[count : 2 * count], rest[2 * count : 3 * count]
        s_pair, s_quad, s_z, sems = rest[3 * count : 3 * count + 3] + (rest[3 * count + 3 :],)
        pair_s, pair_r, quad_s, quad_r, lev_s, lev_r, peer_s, core_s, got_r = sems[:9]
        sp_s, sp_r, sq_s, sq_r, sz_s, sz_r = sems[9:]
        dp, z, y = lax.axis_index("dp"), lax.axis_index("fsdp"), lax.axis_index("ctx")
        core = dp % 2
        mine = dp * halves + y
        chip = (dp // 2) * halves + y

        def group_of(other_chip, other_core):
            return ((other_chip // halves) * 2 + other_core) * halves + other_chip % halves

        def place(group, level):
            return {"dp": group // halves, "fsdp": level, "ctx": group % halves}

        sibling = group_of(chip, 1 - core)

        def peer(hop):
            return group_of((chip + hop) % chips, core)

        barrier = pltpu.get_barrier_semaphore()

        def greet(group, level):
            pl.semaphore_signal(
                barrier, inc=1, device_id=place(group, level), device_id_type=pl.DeviceIdType.MESH
            )

        greet(sibling, z)
        for hop in range(1, chips):
            greet(peer(hop), z)
        for step in range(1, levels):
            greet(mine, (z + step) % levels)
        pl.semaphore_wait(barrier, chips + levels - 1)

        def remote(src, dst, send, recv, group, level):
            return pltpu.make_async_remote_copy(
                src_ref=src, dst_ref=dst, send_sem=send, recv_sem=recv,
                device_id=place(group, level), device_id_type=pl.DeviceIdType.MESH,
            )

        def pair_copy(a, step, other_chip):
            level = (z + step) % levels
            return remote(
                ins[a].at[level * groups + group_of(other_chip, 1 - core)],
                pair_buf[a].at[step, other_chip],
                pair_s.at[a, step, other_chip], pair_r.at[a, step, other_chip], sibling, z,
            )

        def quad_copy(a, step, hop):
            return remote(
                pair_buf[a].at[step, (chip + hop) % chips],
                quad_buf[a].at[step, hop - 1],
                quad_s.at[a, step, hop], quad_r.at[a, step, hop], peer(hop), z,
            )

        def level_copy(a, step):
            return remote(
                pair_buf[a].at[step, chip],
                z_buf[a].at[step - 1],
                lev_s.at[a, step], lev_r.at[a, step], mine, (z + step) % levels,
            )

        def peer_copy(a, hop):
            return remote(
                outs[a].at[mine], outs[a].at[mine], peer_s.at[a, hop], got_r.at[a, mine], peer(hop), z
            )

        def core_copy(a, hop):
            group = peer(hop)
            return remote(
                outs[a].at[group], outs[a].at[group], core_s.at[a, hop], got_r.at[a, group], sibling, z
            )

        def arrived(a, group):
            remote(
                outs[a].at[group], outs[a].at[group], core_s.at[a, 0], got_r.at[a, group], sibling, z
            ).wait_recv()

        small_pair = remote(small_in, s_pair, sp_s, sp_r, sibling, z)

        def small_quad(hop):
            return remote(
                s_quad.at[chip], s_quad.at[chip], sq_s.at[hop], sq_r.at[chip], peer(hop), z
            )

        def small_level(step):
            return remote(
                s_z.at[z], s_z.at[z], sz_s.at[step], sz_r.at[z], mine, (z + step) % levels
            )

        small_pair.start()
        steps = list(range(1, levels)) + [0]
        units = [(a, step) for a in range(count) for step in steps]
        for a, step in units:
            for other in range(chips):
                pair_copy(a, step, other).start()

        small_pair.wait_recv()
        s_quad[chip] = small_in[...] + s_pair[...]

        def pair_sum(a, step):
            level = (z + step) % levels

            def one(other, carry):
                pair_copy(a, step, other).wait_recv()
                own = ins[a][level * groups + group_of(other, core)].astype(wide)
                total = own + pair_buf[a][step, other].astype(wide)
                pair_buf[a][step, other] = total.astype(jnp.bfloat16)
                return carry

            lax.fori_loop(0, chips, one, 0)

        def quad_sum(a, step):
            for hop in range(1, chips):
                quad_copy(a, step, hop).wait_recv()
            total = pair_buf[a][step, chip].astype(wide)
            for hop in range(1, chips):
                total = total + quad_buf[a][step, hop - 1].astype(wide)
            pair_buf[a][step, chip] = total.astype(jnp.bfloat16)

        def level_sum(a):
            for step in range(1, levels):
                level_copy(a, step).wait_recv()
            total = pair_buf[a][0, chip].astype(wide)
            for step in range(1, levels):
                total = total + z_buf[a][step - 1].astype(wide)
            outs[a][mine] = total.astype(jnp.bfloat16)

        lag = 2
        for index in range(len(units) + lag):
            if index < len(units):
                pair_sum(*units[index])
            if index >= lag:
                quad_sum(*units[index - lag])
            if index == 0:
                for hop in range(1, chips):
                    small_quad(hop).start()
            if index < len(units):
                for hop in range(1, chips):
                    quad_copy(*units[index], hop).start()
            if index >= lag and units[index - lag][1] > 0:
                level_copy(*units[index - lag]).start()

        def small_wait_quad(other):
            remote(
                s_quad.at[other], s_quad.at[other], sq_s.at[0], sq_r.at[other], sibling, z
            ).wait_recv()

        for hop in range(1, chips):
            small_wait_quad((chip + hop) % chips)
        total = s_quad[0]
        for other in range(1, chips):
            total = total + s_quad[other]
        s_z[z] = total
        for a in range(count):
            level_sum(a)
            if a == 0:
                for step in range(1, levels):
                    small_level(step).start()
            if a > 0:
                for hop in range(1, chips):
                    peer_copy(a - 1, hop).start()
                core_copy(a - 1, 0).start()

        for step in range(1, levels):
            other = (z + step) % levels
            remote(s_z.at[other], s_z.at[other], sz_s.at[0], sz_r.at[other], sibling, z).wait_recv()
        for hop in range(1, chips):
            peer_copy(count - 1, hop).start()
        core_copy(count - 1, 0).start()
        total = s_z[0]
        for other in range(1, levels):
            total = total + s_z[other]
        small_out[...] = total

        for a in range(count):
            for hop in range(1, chips):
                arrived(a, peer(hop))
                core_copy(a, hop).start()
        for a in range(count):
            for hop in range(chips):
                arrived(a, group_of((chip + hop) % chips, 1 - core))

        small_pair.wait_send()
        for hop in range(1, chips):
            small_quad(hop).wait_send()
        for step in range(1, levels):
            small_level(step).wait_send()
        for a, step in units:
            for other in range(chips):
                pair_copy(a, step, other).wait_send()
            for hop in range(1, chips):
                quad_copy(a, step, hop).wait_send()
            if step > 0:
                level_copy(a, step).wait_send()
        for a in range(count):
            for hop in range(1, chips):
                peer_copy(a, hop).wait_send()
            for hop in range(chips):
                core_copy(a, hop).wait_send()

    dma = pltpu.SemaphoreType.DMA
    shapes = [grad.shape[1:] for grad in grads]
    low = jnp.bfloat16
    vmem = pl.BlockSpec(memory_space=pltpu.VMEM)
    return pl.pallas_call(
        body,
        out_shape=[jax.ShapeDtypeStruct((groups,) + shape, low) for shape in shapes]
        + [jax.ShapeDtypeStruct(small.shape, small.dtype)],
        in_specs=[vmem] * (count + 1),
        out_specs=[vmem] * (count + 1),
        scratch_shapes=[pltpu.VMEM((levels, chips) + shape, low) for shape in shapes]
        + [pltpu.VMEM((levels, chips - 1) + shape, low) for shape in shapes]
        + [pltpu.VMEM((levels - 1,) + shape, low) for shape in shapes]
        + [
            pltpu.VMEM(small.shape, small.dtype),
            pltpu.VMEM((chips,) + small.shape, small.dtype),
            pltpu.VMEM((levels,) + small.shape, small.dtype),
            dma((count, levels, chips)), dma((count, levels, chips)),
            dma((count, levels, chips)), dma((count, levels, chips)),
            dma((count, levels)), dma((count, levels)),
            dma((count, chips)), dma((count, chips)), dma((count, groups)),
            dma, dma, dma((chips,)), dma((chips,)), dma((levels,)), dma((levels,)),
        ],
        compiler_params=pltpu.CompilerParams(
            collective_id=2, has_side_effects=True, vmem_limit_bytes=60 * 1024 * 1024
        ),
        name="reduce_grads",
    )(*grads, small)


def reduce_all(mesh, grads, small):
    pieces = mesh.shape["fsdp"] * mesh.shape["dp"] * mesh.shape["ctx"]
    cut = [
        grad.astype(jnp.bfloat16).reshape(pieces, grad.shape[0] // pieces, grad.shape[1])
        for grad in grads
    ]
    flat = jnp.concatenate(small)
    room = -flat.shape[0] % (8 * LANES)
    flat = jnp.pad(flat, (0, room)).reshape(-1, LANES)
    results = reduce_kernel(mesh, cut, flat)
    owned = [part.reshape(-1, part.shape[2]).astype(jnp.float32) for part in results[:-1]]
    total = results[-1].reshape(-1)
    sums, start = [], 0
    for part in small:
        sums.append(total[start : start + part.shape[0]])
        start += part.shape[0]
    return owned, sums


def prepare(proj, gains, bias, pairs):
    rows = proj.shape[0]
    col = lambda base: pl.BlockSpec((rows, LANES), lambda p: (0, base + p))
    fixed = lambda shape: pl.BlockSpec(shape, lambda p: (0, 0))
    low = jax.ShapeDtypeStruct((rows, pairs * LANES), jnp.bfloat16)
    return pl.pallas_call(
        prep_kernel,
        grid=(pairs,),
        out_shape=[
            low, low, low,
            jax.ShapeDtypeStruct((rows, LANES), jnp.float32),
            jax.ShapeDtypeStruct((TABLE, rows), jnp.float32),
        ],
        in_specs=[
            col(0), col(pairs), col(2 * pairs),
            pl.BlockSpec((rows, LANES), lambda p: (0, 4 * pairs)),
            fixed((1, LANES)), fixed((1, LANES)), fixed((1, LANES)),
        ],
        out_specs=[col(0), col(0), col(0), fixed((rows, LANES)), fixed((TABLE, rows))],
        name="prep",
    )(proj, proj, proj, proj, gains[0], gains[1], bias)


def attend(qn, kn, vb, kp, vp, cum, cumt, cumtp, pairs):
    rows = qn.shape[0]
    col = pl.BlockSpec((rows, LANES), lambda p: (0, p))
    fixed = lambda shape: pl.BlockSpec(shape, lambda p: (0, 0))
    return pl.pallas_call(
        forward_kernel,
        grid=(pairs,),
        out_shape=[
            jax.ShapeDtypeStruct((rows, pairs * LANES), jnp.float32),
            jax.ShapeDtypeStruct((rows, LANES), jnp.float32),
        ],
        in_specs=[col] * 5 + [fixed((rows, LANES)), fixed((TABLE, rows)), fixed((TABLE, rows))],
        out_specs=[col, fixed((rows, LANES))],
        scratch_shapes=[
            pltpu.VMEM((2, rows, LANES), jnp.float32),
            pltpu.VMEM((2, rows, 1), jnp.float32),
        ],
        name="attend",
    )(qn, kn, vb, kp, vp, cum, cumt, cumtp)


def attend_back(qn, kn, vb, kp, vp, grad, rowc, cumt, cumtp, pairs):
    rows = qn.shape[0]
    col = pl.BlockSpec((rows, LANES), lambda p: (0, p))
    fixed = lambda shape: pl.BlockSpec(shape, lambda p: (0, 0))
    wide = jax.ShapeDtypeStruct((rows, pairs * LANES), jnp.float32)
    low = jax.ShapeDtypeStruct((rows, pairs * LANES), jnp.bfloat16)
    shapes = [(rows, LANES), (TABLE, rows), (TABLE, rows + LANES)]
    return pl.pallas_call(
        backward_kernel,
        grid=(pairs,),
        out_shape=[wide, wide, wide, low, low]
        + [jax.ShapeDtypeStruct(shape, jnp.float32) for shape in shapes],
        in_specs=[col] * 6 + [fixed((rows, LANES)), fixed((TABLE, rows)), fixed((TABLE, rows))],
        out_specs=[col] * 5 + [fixed(shape) for shape in shapes],
        scratch_shapes=[pltpu.VMEM((2, rows, LANES), jnp.float32)] * 2,
        name="attend_back",
    )(qn, kn, vb, kp, vp, grad, rowc, cumt, cumtp)


def finish_back(proj, gains, bias, dq, dk, dv, dkr, dvr, dcq, dck, dckr, dog, pairs):
    rows = proj.shape[0]
    at = lambda base: pl.BlockSpec((rows, LANES), lambda p: (0, base + p))
    col = at(0)
    fixed = lambda shape: pl.BlockSpec(shape, lambda p: (0, 0))
    total = (4 * pairs + 1) * LANES
    return pl.pallas_call(
        post_kernel,
        grid=(pairs,),
        out_shape=[
            jax.ShapeDtypeStruct((rows, total), jnp.bfloat16),
            jax.ShapeDtypeStruct((8, LANES), jnp.float32),
            jax.ShapeDtypeStruct((8, LANES), jnp.float32),
        ],
        in_specs=[
            at(0), at(pairs), pl.BlockSpec((rows, LANES), lambda p: (0, 4 * pairs)),
            fixed((1, LANES)), fixed((1, LANES)), fixed((1, LANES)),
            col, col, col, col, col,
            fixed((rows, LANES)), fixed((TABLE, rows)), fixed((TABLE, rows + LANES)), col,
        ],
        out_specs=[fixed((rows, total)), fixed((8, LANES)), fixed((8, LANES))],
        scratch_shapes=[pltpu.VMEM((LANES, rows), jnp.float32)],
        name="finish_back",
    )(proj, proj, proj, gains[0], gains[1], bias, dq, dk, dv, dkr, dvr, dcq, dck, dckr, dog)


def shards(
    mesh,
    tokens,
    cotangent,
    w_qkv,
    w_forget,
    w_ogate,
    w_out,
    w_gu,
    w_down,
    norm_attn,
    norm_ffn,
    query_gain,
    key_gain,
    forget_bias,
    ogate_bias,
):
    inputs = tokens[0].astype(jnp.float32)
    grad_top = cotangent[0].astype(jnp.float32)
    grad_low = cotangent[0]
    rows, width = inputs.shape
    heads = forget_bias.shape[0]
    pairs = width // LANES
    hidden = w_gu.shape[1] // 2
    groups = mesh.shape["dp"] * mesh.shape["ctx"]
    levels = mesh.shape["fsdp"]
    cut = lambda shard: shard.reshape(groups, shard.shape[0] // groups, shard.shape[1])
    forget_wide = jnp.pad(w_forget, ((0, 0), (0, LANES - heads)))
    first = cut(jnp.concatenate([w_qkv, w_ogate, forget_wide], axis=1))
    second = cut(jnp.concatenate([w_out, w_gu], axis=1))
    proj_full, mid_full, down_full = (
        full.reshape(-1, full.shape[2]) for full in gather_weights(mesh, (first, second, cut(w_down)))
    )
    out_full, gu_full = mid_full[:, :width], mid_full[:, width:]

    factor_one = rms_factor(inputs)
    act_one = (inputs * factor_one * norm_attn).astype(jnp.bfloat16)
    proj = jnp.dot(act_one, proj_full, preferred_element_type=jnp.float32)
    gains = tuple(jnp.concatenate([gain, gain])[None] for gain in (query_gain, key_gain))
    bias = jnp.pad(forget_bias, (0, LANES - heads))[None]
    qn, kn, vb, cum, cumt = prepare(proj, gains, bias, pairs)
    kp, vp, cumtp = (lax.ppermute(part, "ctx", [(0, 1)]) for part in (kn, vb, cumt))
    attn, rowc = attend(qn, kn, vb, kp, vp, cum, cumt, cumtp, pairs)
    ogate = jax.nn.sigmoid(proj[:, 3 * width : 4 * width] + ogate_bias)
    gated = (attn * ogate).astype(jnp.bfloat16)
    middle = inputs + jnp.dot(gated, out_full, preferred_element_type=jnp.float32)
    factor_two = rms_factor(middle)
    act_two = (middle * factor_two * norm_ffn).astype(jnp.bfloat16)
    gate_up = jnp.dot(act_two, gu_full, preferred_element_type=jnp.float32)
    gate_part = gate_up[:, :hidden]
    up_part = gate_up[:, hidden:]
    hidden_low = (jax.nn.silu(gate_part) * up_part).astype(jnp.bfloat16)
    result = middle + jnp.dot(hidden_low, down_full, preferred_element_type=jnp.float32)

    grad_down = inner_rows(hidden_low, grad_low)
    grad_hidden = times_trans(grad_low, down_full)
    sigma = jax.nn.sigmoid(gate_part)
    grad_gu_low = jnp.concatenate(
        [
            grad_hidden * up_part * sigma * (1.0 + gate_part * (1.0 - sigma)),
            grad_hidden * (gate_part * sigma),
        ],
        axis=1,
    ).astype(jnp.bfloat16)
    grad_gu = inner_rows(act_two, grad_gu_low)
    grad_act_two = times_trans(grad_gu_low, gu_full)
    grad_norm_ffn = jnp.sum(grad_act_two * middle * factor_two, axis=0)
    grad_middle = grad_top + rms_back(middle, factor_two, grad_act_two, norm_ffn)
    middle_low = grad_middle.astype(jnp.bfloat16)
    grad_out = inner_rows(gated, middle_low)
    grad_gated = times_trans(middle_low, out_full)
    grad_attn_low = (grad_gated * ogate).astype(jnp.bfloat16)
    grad_ogate_pre = grad_gated * attn * ogate * (1.0 - ogate)
    grad_ogate_bias = jnp.sum(grad_ogate_pre, axis=0)
    ogate_low = grad_ogate_pre.astype(jnp.bfloat16)

    dq, dk, dv, dkp, dvp, dcq, dck, dckp = attend_back(
        qn, kn, vb, kp, vp, grad_attn_low, rowc, cumt, cumtp, pairs
    )
    dkr, dvr, dckr = (lax.ppermute(part, "ctx", [(1, 0)]) for part in (dkp, dvp, dckp))
    proj_low, gain_sums, bias_sums = finish_back(
        proj, gains, bias, dq, dk, dv, dkr, dvr, dcq, dck, dckr, ogate_low, pairs
    )
    grad_proj = inner_rows(act_one, proj_low)
    grad_act_one = times_trans(proj_low, proj_full)
    grad_norm_attn = jnp.sum(grad_act_one * inputs * factor_one, axis=0)
    grad_inputs = grad_middle + rms_back(inputs, factor_one, grad_act_one, norm_attn)

    small = (
        grad_norm_attn,
        grad_norm_ffn,
        gain_sums[0, :HALF] + gain_sums[0, HALF:],
        gain_sums[1, :HALF] + gain_sums[1, HALF:],
        bias_sums[0, :heads],
        grad_ogate_bias,
    )
    owned, small = reduce_all(mesh, (grad_proj, grad_out, grad_gu, grad_down), small)
    own_proj, own_out, own_gu, own_down = owned
    return (
        result[None],
        grad_inputs[None],
        own_proj[:, : 3 * width],
        own_proj[:, 4 * width : 4 * width + heads],
        own_proj[:, 3 * width : 4 * width],
        own_out,
        own_gu,
        own_down,
    ) + tuple(small)


def solution(mesh):
    block = P(("dp", "fsdp"), "ctx", None)
    rows = P("fsdp", None)
    return jax.shard_map(
        functools.partial(shards, mesh),
        mesh=mesh,
        in_specs=(block, block) + (rows,) * 6 + (P(),) * 6,
        out_specs=(block, block) + (rows,) * 6 + (P(),) * 6,
        check_vma=False,
    )
```

```python
import functools

import jax
import jax.numpy as jnp
from jax import lax
from jax.experimental import pallas as pl
from jax.experimental.pallas import tpu as pltpu
from jax.sharding import PartitionSpec as P

EPS = 1e-06
NEG_FILL = -1e30
LANES = 128
HALF = 64
TABLE = 16


def rms_factor(values):
    return lax.rsqrt(jnp.mean(values * values, axis=-1, keepdims=True) + EPS)


def rms_back(values, factor, grad_normed, gain):
    scaled = grad_normed * gain
    inner = jnp.mean(scaled * values, axis=-1, keepdims=True)
    return factor * scaled - factor * factor * factor * values * inner


def inner_rows(left, right):
    return lax.dot_general(
        left, right, (((0,), (0,)), ((), ())), preferred_element_type=jnp.float32
    )


def times_trans(left, right):
    return lax.dot_general(
        left, right, (((1,), (1,)), ((), ())), preferred_element_type=jnp.float32
    )


def lane_ids(rows):
    return lax.broadcasted_iota(jnp.int32, (rows, LANES), 1)


def head_half(pair_block, half):
    lanes = lane_ids(pair_block.shape[0])
    inside = (lanes < HALF) if half == 0 else (lanes >= HALF)
    return jnp.where(inside, pair_block, jnp.zeros_like(pair_block))


def both_halves(low, high):
    return jnp.where(lane_ids(low.shape[0]) < HALF, low, high)


def half_sums(values):
    lanes = lane_ids(values.shape[0])
    low = jnp.sum(jnp.where(lanes < HALF, values, 0.0), axis=1, keepdims=True)
    high = jnp.sum(jnp.where(lanes >= HALF, values, 0.0), axis=1, keepdims=True)
    return jnp.where(lanes < HALF, low, high)


def head_column(table, head):
    return jnp.sum(jnp.where(lane_ids(table.shape[0]) == head, table, 0.0), axis=1, keepdims=True)


def running_sum(values, reverse):
    rows = values.shape[0]
    at = lax.broadcasted_iota(jnp.int32, values.shape, 0)
    step = 1
    while step < rows:
        if reverse:
            moved = pltpu.roll(values, rows - step, 0)
            values = values + jnp.where(at < rows - step, moved, 0.0)
        else:
            moved = pltpu.roll(values, step, 0)
            values = values + jnp.where(at >= step, moved, 0.0)
        step *= 2
    return values


def log_sigmoid(values):
    return jnp.minimum(values, 0.0) - jnp.log(1.0 + jnp.exp(-jnp.abs(values)))


def prep_kernel(q_ref, k_ref, v_ref, f_ref, gq_ref, gk_ref, bias_ref, qn_ref, kn_ref, vb_ref, cum_ref, cumt_ref):
    query = q_ref[...]
    factor = lax.rsqrt(half_sums(query * query) * (1.0 / HALF) + EPS)
    low = (query * factor * gq_ref[...]).astype(jnp.bfloat16)
    qn_ref[...] = (low.astype(jnp.float32) * HALF ** (-0.5)).astype(jnp.bfloat16)
    keys = k_ref[...]
    factor = lax.rsqrt(half_sums(keys * keys) * (1.0 / HALF) + EPS)
    kn_ref[...] = (keys * factor * gk_ref[...]).astype(jnp.bfloat16)
    vb_ref[...] = v_ref[...].astype(jnp.bfloat16)

    @pl.when(pl.program_id(0) == 0)
    def _():
        cum = running_sum(log_sigmoid(f_ref[...] + bias_ref[...]), False)
        cum_ref[...] = cum
        cumt_ref[...] = cum.T[: cumt_ref.shape[0]]


def weigh(q_half, k_block, row_term, col_term, masked):
    scores = times_trans(q_half, k_block) + row_term - col_term
    if masked:
        rows = lax.broadcasted_iota(jnp.int32, scores.shape, 0)
        cols = lax.broadcasted_iota(jnp.int32, scores.shape, 1)
        scores = jnp.where(cols <= rows, scores, NEG_FILL)
    return jnp.exp(scores)


def forward_kernel(q_ref, k_ref, v_ref, kp_ref, vp_ref, cum_ref, cumt_ref, cumtp_ref, o_ref, rowc_ref, acc, tot):
    pair = pl.program_id(0)
    rows = q_ref.shape[0]
    block = rows // 2
    past = lax.axis_index("ctx") > 0

    @pl.when(pair == 0)
    def _():
        rowc_ref[...] = jnp.zeros_like(rowc_ref)

    for half in range(2):
        head = 2 * pair + half
        col = cumt_ref[pl.ds(head, 1), :]
        for qb in range(2):
            span = slice(qb * block, (qb + 1) * block)
            row = head_column(cum_ref[span, :], head)
            q_half = head_half(q_ref[span, :], half)
            weights = weigh(q_half, k_ref[span, :], row, col[:, span], True)
            total = jnp.sum(weights, axis=1, keepdims=True)
            attended = jnp.dot(
                weights.astype(jnp.bfloat16), v_ref[span, :], preferred_element_type=jnp.float32
            )
            if qb == 1:
                weights = weigh(q_half, k_ref[:block, :], row, col[:, :block], False)
                total = total + jnp.sum(weights, axis=1, keepdims=True)
                attended = attended + jnp.dot(
                    weights.astype(jnp.bfloat16), v_ref[:block, :], preferred_element_type=jnp.float32
                )
            acc[half, span, :] = attended
            tot[half, span, :] = total

    @pl.when(past)
    def _():
        for half in range(2):
            head = 2 * pair + half
            col = cumtp_ref[pl.ds(head, 1), :]
            col = col - col[:, rows - 1 : rows]
            for qb in range(2):
                span = slice(qb * block, (qb + 1) * block)
                row = head_column(cum_ref[span, :], head)
                q_half = head_half(q_ref[span, :], half)
                weights = weigh(q_half, kp_ref[...], row, col, False)
                acc[half, span, :] += jnp.dot(
                    weights.astype(jnp.bfloat16), vp_ref[...], preferred_element_type=jnp.float32
                )
                tot[half, span, :] += jnp.sum(weights, axis=1, keepdims=True)

    o_ref[...] = both_halves(acc[0] / tot[0], acc[1] / tot[1])
    lanes = lane_ids(rows)
    table = rowc_ref[...]
    for half in range(2):
        head = 2 * pair + half
        row = head_column(cum_ref[...], head) - jnp.log(tot[half])
        table = jnp.where(lanes == head, row, table)
    rowc_ref[...] = table


def backward_kernel(
    q_ref, k_ref, v_ref, kp_ref, vp_ref, do_ref, rowc_ref, cumt_ref, cumtp_ref,
    dq_ref, dk_ref, dv_ref, dkp_ref, dvp_ref, dcq_ref, dck_ref, dckp_ref, kacc, vacc,
):
    pair = pl.program_id(0)
    rows = q_ref.shape[0]
    block = rows // 2
    rank = lax.axis_index("ctx")

    @pl.when(pair == 0)
    def _():
        dcq_ref[...] = jnp.zeros_like(dcq_ref)
        dck_ref[...] = jnp.zeros_like(dck_ref)
        dckp_ref[...] = jnp.zeros_like(dckp_ref)

    def run(with_past):
        kacc[...] = jnp.zeros_like(kacc)
        vacc[...] = jnp.zeros_like(vacc)
        for half in range(2):
            head = 2 * pair + half
            col = cumt_ref[pl.ds(head, 1), :]
            if with_past:
                colp = cumtp_ref[pl.ds(head, 1), :]
                colp = colp - colp[:, rows - 1 : rows]
            down_total = jnp.zeros((1, 1), jnp.float32)
            for qb in range(2):
                span = slice(qb * block, (qb + 1) * block)
                row = head_column(rowc_ref[span, :], head)
                q_half = head_half(q_ref[span, :], half)
                do_half = head_half(do_ref[span, :], half)
                pieces = [(k_ref, v_ref, span, col[:, span], True, 0)]
                if qb == 1:
                    pieces.append((k_ref, v_ref, slice(0, block), col[:, :block], False, 0))
                if with_past:
                    for kb in range(2):
                        part = slice(kb * block, (kb + 1) * block)
                        pieces.append((kp_ref, vp_ref, part, colp[:, part], False, 1))
                probs, grads = [], []
                delta = jnp.zeros((block, 1), jnp.float32)
                for keys, values, part, cols, masked, where in pieces:
                    prob = weigh(q_half, keys[part, :], row, cols, masked)
                    grad = times_trans(do_half, values[part, :])
                    delta = delta + jnp.sum(prob * grad, axis=1, keepdims=True)
                    vacc[where, part, :] += inner_rows(prob.astype(jnp.bfloat16), do_half)
                    probs.append(prob)
                    grads.append(grad)
                query_grad = jnp.zeros((block, LANES), jnp.float32)
                row_sum = jnp.zeros((block, 1), jnp.float32)
                for (keys, values, part, cols, masked, where), prob, grad in zip(pieces, probs, grads):
                    score_grad = prob * (grad - delta)
                    low = score_grad.astype(jnp.bfloat16)
                    query_grad = query_grad + jnp.dot(
                        low, keys[part, :], preferred_element_type=jnp.float32
                    )
                    kacc[where, part, :] += inner_rows(low, q_half)
                    row_sum = row_sum + jnp.sum(score_grad, axis=1, keepdims=True)
                    col_sum = jnp.sum(score_grad, axis=0, keepdims=True)
                    target = dckp_ref if where else dck_ref
                    target[pl.ds(head, 1), part] += -col_sum
                    if not where:
                        down_total = down_total - jnp.sum(col_sum, axis=1, keepdims=True)
                query_grad = query_grad * HALF ** (-0.5)
                if half == 0:
                    dq_ref[span, :] = query_grad
                else:
                    dq_ref[span, :] = both_halves(dq_ref[span, :], query_grad)
                dcq_ref[span, :] = jnp.where(lane_ids(block) == head, row_sum, dcq_ref[span, :])
                down_total = down_total + jnp.sum(row_sum, axis=0, keepdims=True)
            table = dckp_ref[:, rows:]
            at = lax.broadcasted_iota(jnp.int32, table.shape, 0)
            dckp_ref[:, rows:] = jnp.where(at == head, down_total, table)
        dk_ref[...] = kacc[0]
        dv_ref[...] = vacc[0]
        dkp_ref[...] = kacc[1].astype(jnp.bfloat16)
        dvp_ref[...] = vacc[1].astype(jnp.bfloat16)

    @pl.when(rank == 0)
    def _():
        run(False)

    @pl.when(rank > 0)
    def _():
        run(True)


def rms_back_pair(values, grad, gain):
    factor = lax.rsqrt(half_sums(values * values) * (1.0 / HALF) + EPS)
    scaled = grad * gain
    inner = half_sums(scaled * values) * (1.0 / HALF)
    gain_grad = jnp.sum(grad * values * factor, axis=0, keepdims=True)
    return factor * scaled - factor * factor * factor * values * inner, gain_grad


def post_kernel(
    q_ref, k_ref, f_ref, gq_ref, gk_ref, bias_ref, dq_ref, dk_ref, dv_ref, dkr_ref, dvr_ref,
    dcq_ref, dck_ref, dckr_ref, dog_ref, out_ref, gains_ref, dbias_ref, flip,
):
    pair = pl.program_id(0)
    pairs = pl.num_programs(0)
    rows = q_ref.shape[0]
    width = pairs * LANES

    def place(base):
        return pl.ds(pl.multiple_of(base + pair * LANES, LANES), LANES)

    grad, query_gain = rms_back_pair(q_ref[...], dq_ref[...], gq_ref[...])
    out_ref[:, place(0)] = grad.astype(jnp.bfloat16)
    key_grad = dk_ref[...] + dkr_ref[...].astype(jnp.float32)
    grad, key_gain = rms_back_pair(k_ref[...], key_grad, gk_ref[...])
    out_ref[:, place(width)] = grad.astype(jnp.bfloat16)
    out_ref[:, place(2 * width)] = (dv_ref[...] + dvr_ref[...].astype(jnp.float32)).astype(jnp.bfloat16)
    out_ref[:, place(3 * width)] = dog_ref[...]

    @pl.when(pair == 0)
    def _():
        gains_ref[...] = jnp.zeros_like(gains_ref)
        count = dck_ref.shape[0]
        flip[...] = jnp.zeros_like(flip)
        flip[:count, :] = dck_ref[...] + dckr_ref[:, :rows]
        cum_grad = dcq_ref[...] + flip[...].T
        flip[...] = jnp.zeros_like(flip)
        flip[:count, :LANES] = dckr_ref[:, rows:]
        later = flip[:, :LANES].T[:1, :]
        log_grad = running_sum(cum_grad, True) + later
        gate = f_ref[...] + bias_ref[...]
        gate_grad = log_grad * jax.nn.sigmoid(-gate)
        dbias_ref[...] = jnp.broadcast_to(jnp.sum(gate_grad, axis=0, keepdims=True), dbias_ref.shape)
        out_ref[:, 4 * width :] = gate_grad.astype(jnp.bfloat16)

    gains_ref[0:1, :] += query_gain
    gains_ref[1:2, :] += key_gain


def gather_weights(mesh, pieces, call):
    groups, levels, halves = mesh.shape["dp"] * mesh.shape["ctx"], mesh.shape["fsdp"], mesh.shape["ctx"]
    count = len(pieces)
    chips = groups // 2

    def body(*refs):
        ins, outs = refs[:count], refs[count : 2 * count]
        keep_sem, z_sem, peer_sem, core_sem, got_sem = refs[2 * count :]
        dp, z, y = lax.axis_index("dp"), lax.axis_index("fsdp"), lax.axis_index("ctx")
        core = dp % 2
        mine = dp * halves + y
        chip = (dp // 2) * halves + y

        def group_of(other_chip, other_core):
            return ((other_chip // halves) * 2 + other_core) * halves + other_chip % halves

        def place(group, level):
            return {"dp": group // halves, "fsdp": level, "ctx": group % halves}

        barrier = pltpu.get_barrier_semaphore()

        def greet(group, level):
            pl.semaphore_signal(
                barrier, inc=1, device_id=place(group, level), device_id_type=pl.DeviceIdType.MESH
            )

        sibling = group_of(chip, 1 - core)
        greet(sibling, z)
        for hop in range(1, chips):
            greet(group_of((chip + hop) % chips, core), z)

        @pl.when(z > 0)
        def _():
            greet(mine, z - 1)

        @pl.when(z < levels - 1)
        def _():
            greet(mine, z + 1)

        ends = jnp.minimum(z, 1) + jnp.minimum(levels - 1 - z, 1)
        pl.semaphore_wait(barrier, chips + ends)

        def copy(a, level, group, to_group, to_level, sem, own=False):
            slot = level * groups + group
            return pltpu.make_async_remote_copy(
                src_ref=ins[a].at[group] if own else outs[a].at[slot],
                dst_ref=outs[a].at[slot],
                send_sem=sem,
                recv_sem=got_sem.at[a, slot],
                device_id=place(to_group, to_level),
                device_id_type=pl.DeviceIdType.MESH,
            )

        def z_copy(a, level, side, own=False):
            return copy(a, level, mine, mine, z + (1 if side else -1), z_sem.at[a, level, side], own)

        def peer_copy(a, level, hop):
            return copy(a, level, mine, group_of((chip + hop) % chips, core), z, peer_sem.at[a, level, hop])

        def core_copy(a, level, hop):
            return copy(a, level, group_of((chip + hop) % chips, core), sibling, z, core_sem.at[a, level, hop])

        def arrived(a, level, group):
            copy(a, level, group, sibling, z, core_sem.at[a, level, 0]).wait_recv()

        def kept(a):
            return pltpu.make_async_copy(ins[a], outs[a].at[pl.ds(z * groups, groups)], keep_sem.at[a])

        def edges(action):
            for a in range(count):

                @pl.when(z < levels - 1)
                def _():
                    action(z_copy(a, z, 1, True))

                @pl.when(z > 0)
                def _():
                    action(z_copy(a, z, 0, True))

        edges(lambda item: item.start())
        for a in range(count):
            kept(a).start()

        def near(a, level, side, last):
            arrived(a, level, mine)

            @pl.when(jnp.logical_not(last))
            def _():
                z_copy(a, level, side).start()

            for hop in range(1, chips):
                peer_copy(a, level, hop).start()
            core_copy(a, level, 0).start()

        for a in range(count):
            for step in range(1, levels):

                @pl.when(z - step >= 0)
                def _():
                    near(a, z - step, 1, z == levels - 1)

                @pl.when(z + step < levels)
                def _():
                    near(a, z + step, 0, z == 0)

        def others(action):
            for a in range(count):
                for step in range(1, levels):
                    level = (z + step) % levels
                    action(a, level)

        def spread(a, level):
            for hop in range(1, chips):
                arrived(a, level, group_of((chip + hop) % chips, core))
                core_copy(a, level, hop).start()

        def finish(a, level):
            for hop in range(chips):
                arrived(a, level, group_of((chip + hop) % chips, 1 - core))
            for hop in range(chips):
                core_copy(a, level, hop).wait_send()
            for hop in range(1, chips):
                peer_copy(a, level, hop).wait_send()

        others(spread)
        others(finish)
        edges(lambda item: item.wait_send())
        for a in range(count):
            kept(a).wait()
            for step in range(1, levels):

                @pl.when(jnp.logical_and(z - step >= 0, z < levels - 1))
                def _():
                    z_copy(a, z - step, 1).wait_send()

                @pl.when(jnp.logical_and(z + step < levels, z > 0))
                def _():
                    z_copy(a, z + step, 0).wait_send()

    dma = pltpu.SemaphoreType.DMA
    return pl.pallas_call(
        body,
        out_shape=[
            jax.ShapeDtypeStruct((levels * groups,) + piece.shape[1:], piece.dtype) for piece in pieces
        ],
        in_specs=[pl.BlockSpec(memory_space=pltpu.VMEM)] * count,
        out_specs=[pl.BlockSpec(memory_space=pl.ANY)] * count,
        scratch_shapes=[
            dma((count,)),
            dma((count, levels, 2)),
            dma((count, levels, chips)),
            dma((count, levels, chips)),
            dma((count, levels * groups)),
        ],
        compiler_params=pltpu.CompilerParams(collective_id=call, has_side_effects=True),
        cost_estimate=pl.CostEstimate(
            flops=0, bytes_accessed=20 * levels * sum(p.size for p in pieces), transcendentals=0
        ),
        name="gather_weights",
    )(*pieces)


def reduce_kernel(mesh, grads, small, call):
    halves, levels = mesh.shape["ctx"], mesh.shape["fsdp"]
    groups = mesh.shape["dp"] * halves
    chips = groups // 2
    count = len(grads)
    wide = jnp.float32

    def body(*refs):
        ins, small_in = refs[:count], refs[count]
        outs, small_out = refs[count + 1 : 2 * count + 1], refs[2 * count + 1]
        rest = refs[2 * count + 2 :]
        pair_buf, quad_buf, z_buf = rest[:count], rest[count : 2 * count], rest[2 * count : 3 * count]
        s_pair, s_quad, s_z, sems = rest[3 * count : 3 * count + 3] + (rest[3 * count + 3 :],)
        pair_s, pair_r, quad_s, quad_r, lev_s, lev_r, peer_s, core_s, got_r = sems[:9]
        sp_s, sp_r, sq_s, sq_r, sz_s, sz_r = sems[9:]
        dp, z, y = lax.axis_index("dp"), lax.axis_index("fsdp"), lax.axis_index("ctx")
        core = dp % 2
        mine = dp * halves + y
        chip = (dp // 2) * halves + y

        def group_of(other_chip, other_core):
            return ((other_chip // halves) * 2 + other_core) * halves + other_chip % halves

        def place(group, level):
            return {"dp": group // halves, "fsdp": level, "ctx": group % halves}

        sibling = group_of(chip, 1 - core)

        def peer(hop):
            return group_of((chip + hop) % chips, core)

        barrier = pltpu.get_barrier_semaphore()

        def greet(group, level):
            pl.semaphore_signal(
                barrier, inc=1, device_id=place(group, level), device_id_type=pl.DeviceIdType.MESH
            )

        greet(sibling, z)
        for hop in range(1, chips):
            greet(peer(hop), z)
        for step in range(1, levels):
            greet(mine, (z + step) % levels)
        pl.semaphore_wait(barrier, chips + levels - 1)

        def remote(src, dst, send, recv, group, level):
            return pltpu.make_async_remote_copy(
                src_ref=src, dst_ref=dst, send_sem=send, recv_sem=recv,
                device_id=place(group, level), device_id_type=pl.DeviceIdType.MESH,
            )

        def pair_copy(a, step, other_chip):
            level = (z + step) % levels
            return remote(
                ins[a].at[level * groups + group_of(other_chip, 1 - core)],
                pair_buf[a].at[step, other_chip],
                pair_s.at[a, step, other_chip], pair_r.at[a, step, other_chip], sibling, z,
            )

        def quad_copy(a, step, hop):
            return remote(
                pair_buf[a].at[step, (chip + hop) % chips],
                quad_buf[a].at[step, hop - 1],
                quad_s.at[a, step, hop], quad_r.at[a, step, hop], peer(hop), z,
            )

        def level_copy(a, step):
            return remote(
                pair_buf[a].at[step, chip],
                z_buf[a].at[step - 1],
                lev_s.at[a, step], lev_r.at[a, step], mine, (z + step) % levels,
            )

        def peer_copy(a, hop):
            return remote(
                outs[a].at[mine], outs[a].at[mine], peer_s.at[a, hop], got_r.at[a, mine], peer(hop), z
            )

        def core_copy(a, hop):
            group = peer(hop)
            return remote(
                outs[a].at[group], outs[a].at[group], core_s.at[a, hop], got_r.at[a, group], sibling, z
            )

        def arrived(a, group):
            remote(
                outs[a].at[group], outs[a].at[group], core_s.at[a, 0], got_r.at[a, group], sibling, z
            ).wait_recv()

        small_pair = remote(small_in, s_pair, sp_s, sp_r, sibling, z)

        def small_quad(hop):
            return remote(
                s_quad.at[chip], s_quad.at[chip], sq_s.at[hop], sq_r.at[chip], peer(hop), z
            )

        def small_level(step):
            return remote(
                s_z.at[z], s_z.at[z], sz_s.at[step], sz_r.at[z], mine, (z + step) % levels
            )

        small_pair.start()
        steps = list(range(1, levels)) + [0]
        units = [(a, step) for a in range(count) for step in steps]
        for a, step in units:
            for other in range(chips):
                pair_copy(a, step, other).start()

        small_pair.wait_recv()
        s_quad[chip] = small_in[...] + s_pair[...]

        def pair_sum(a, step):
            level = (z + step) % levels

            def one(other, carry):
                pair_copy(a, step, other).wait_recv()
                own = ins[a][level * groups + group_of(other, core)].astype(wide)
                total = own + pair_buf[a][step, other].astype(wide)
                pair_buf[a][step, other] = total.astype(jnp.bfloat16)
                return carry

            lax.fori_loop(0, chips, one, 0)

        def quad_sum(a, step):
            for hop in range(1, chips):
                quad_copy(a, step, hop).wait_recv()
            total = pair_buf[a][step, chip].astype(wide)
            for hop in range(1, chips):
                total = total + quad_buf[a][step, hop - 1].astype(wide)
            pair_buf[a][step, chip] = total.astype(jnp.bfloat16)

        def level_sum(a):
            for step in range(1, levels):
                level_copy(a, step).wait_recv()
            total = pair_buf[a][0, chip].astype(wide)
            for step in range(1, levels):
                total = total + z_buf[a][step - 1].astype(wide)
            outs[a][mine] = total.astype(jnp.bfloat16)

        lag = 2
        for index in range(len(units) + lag):
            if index < len(units):
                pair_sum(*units[index])
            if index >= lag:
                quad_sum(*units[index - lag])
            if index == 0:
                for hop in range(1, chips):
                    small_quad(hop).start()
            if index < len(units):
                for hop in range(1, chips):
                    quad_copy(*units[index], hop).start()
            if index >= lag and units[index - lag][1] > 0:
                level_copy(*units[index - lag]).start()

        def small_wait_quad(other):
            remote(
                s_quad.at[other], s_quad.at[other], sq_s.at[0], sq_r.at[other], sibling, z
            ).wait_recv()

        for hop in range(1, chips):
            small_wait_quad((chip + hop) % chips)
        total = s_quad[0]
        for other in range(1, chips):
            total = total + s_quad[other]
        s_z[z] = total
        for a in range(count):
            level_sum(a)
            if a == 0:
                for step in range(1, levels):
                    small_level(step).start()
            if a > 0:
                for hop in range(1, chips):
                    peer_copy(a - 1, hop).start()
                core_copy(a - 1, 0).start()

        for step in range(1, levels):
            other = (z + step) % levels
            remote(s_z.at[other], s_z.at[other], sz_s.at[0], sz_r.at[other], sibling, z).wait_recv()
        for hop in range(1, chips):
            peer_copy(count - 1, hop).start()
        core_copy(count - 1, 0).start()
        total = s_z[0]
        for other in range(1, levels):
            total = total + s_z[other]
        small_out[...] = total

        for a in range(count):
            for hop in range(1, chips):
                arrived(a, peer(hop))
                core_copy(a, hop).start()
        for a in range(count):
            for hop in range(chips):
                arrived(a, group_of((chip + hop) % chips, 1 - core))

        small_pair.wait_send()
        for hop in range(1, chips):
            small_quad(hop).wait_send()
        for step in range(1, levels):
            small_level(step).wait_send()
        for a, step in units:
            for other in range(chips):
                pair_copy(a, step, other).wait_send()
            for hop in range(1, chips):
                quad_copy(a, step, hop).wait_send()
            if step > 0:
                level_copy(a, step).wait_send()
        for a in range(count):
            for hop in range(1, chips):
                peer_copy(a, hop).wait_send()
            for hop in range(chips):
                core_copy(a, hop).wait_send()

    dma = pltpu.SemaphoreType.DMA
    shapes = [grad.shape[1:] for grad in grads]
    low = jnp.bfloat16
    vmem = pl.BlockSpec(memory_space=pltpu.VMEM)
    return pl.pallas_call(
        body,
        out_shape=[jax.ShapeDtypeStruct((groups,) + shape, low) for shape in shapes]
        + [jax.ShapeDtypeStruct(small.shape, small.dtype)],
        in_specs=[vmem] * (count + 1),
        out_specs=[vmem] * (count + 1),
        scratch_shapes=[pltpu.VMEM((levels, chips) + shape, low) for shape in shapes]
        + [pltpu.VMEM((levels, chips - 1) + shape, low) for shape in shapes]
        + [pltpu.VMEM((levels - 1,) + shape, low) for shape in shapes]
        + [
            pltpu.VMEM(small.shape, small.dtype),
            pltpu.VMEM((chips,) + small.shape, small.dtype),
            pltpu.VMEM((levels,) + small.shape, small.dtype),
            dma((count, levels, chips)), dma((count, levels, chips)),
            dma((count, levels, chips)), dma((count, levels, chips)),
            dma((count, levels)), dma((count, levels)),
            dma((count, chips)), dma((count, chips)), dma((count, groups)),
            dma, dma, dma((chips,)), dma((chips,)), dma((levels,)), dma((levels,)),
        ],
        compiler_params=pltpu.CompilerParams(
            collective_id=call, has_side_effects=True, vmem_limit_bytes=60 * 1024 * 1024
        ),
        cost_estimate=pl.CostEstimate(
            flops=0, bytes_accessed=20 * sum(grad.size for grad in grads), transcendentals=0
        ),
        name="reduce_grads",
    )(*grads, small)


def reduce_all(mesh, grads, small, call):
    pieces = mesh.shape["fsdp"] * mesh.shape["dp"] * mesh.shape["ctx"]
    cut = [
        grad.astype(jnp.bfloat16).reshape(pieces, grad.shape[0] // pieces, grad.shape[1])
        for grad in grads
    ]
    flat = jnp.concatenate(small)
    room = -flat.shape[0] % (8 * LANES)
    flat = jnp.pad(flat, (0, room)).reshape(-1, LANES)
    results = reduce_kernel(mesh, cut, flat, call)
    owned = [part.reshape(-1, part.shape[2]).astype(jnp.float32) for part in results[:-1]]
    total = results[-1].reshape(-1)
    sums, start = [], 0
    for part in small:
        sums.append(total[start : start + part.shape[0]])
        start += part.shape[0]
    return owned, sums


def prepare(proj, gains, bias, pairs):
    rows = proj.shape[0]
    col = lambda base: pl.BlockSpec((rows, LANES), lambda p: (0, base + p))
    fixed = lambda shape: pl.BlockSpec(shape, lambda p: (0, 0))
    low = jax.ShapeDtypeStruct((rows, pairs * LANES), jnp.bfloat16)
    return pl.pallas_call(
        prep_kernel,
        grid=(pairs,),
        out_shape=[
            low, low, low,
            jax.ShapeDtypeStruct((rows, LANES), jnp.float32),
            jax.ShapeDtypeStruct((TABLE, rows), jnp.float32),
        ],
        in_specs=[
            col(0), col(pairs), col(2 * pairs),
            pl.BlockSpec((rows, LANES), lambda p: (0, 4 * pairs)),
            fixed((1, LANES)), fixed((1, LANES)), fixed((1, LANES)),
        ],
        out_specs=[col(0), col(0), col(0), fixed((rows, LANES)), fixed((TABLE, rows))],
        name="prep",
    )(proj, proj, proj, proj, gains[0], gains[1], bias)


def attend(qn, kn, vb, kp, vp, cum, cumt, cumtp, pairs):
    rows = qn.shape[0]
    col = pl.BlockSpec((rows, LANES), lambda p: (0, p))
    fixed = lambda shape: pl.BlockSpec(shape, lambda p: (0, 0))
    return pl.pallas_call(
        forward_kernel,
        grid=(pairs,),
        out_shape=[
            jax.ShapeDtypeStruct((rows, pairs * LANES), jnp.float32),
            jax.ShapeDtypeStruct((rows, LANES), jnp.float32),
        ],
        in_specs=[col] * 5 + [fixed((rows, LANES)), fixed((TABLE, rows)), fixed((TABLE, rows))],
        out_specs=[col, fixed((rows, LANES))],
        scratch_shapes=[
            pltpu.VMEM((2, rows, LANES), jnp.float32),
            pltpu.VMEM((2, rows, 1), jnp.float32),
        ],
        name="attend",
    )(qn, kn, vb, kp, vp, cum, cumt, cumtp)


def attend_back(qn, kn, vb, kp, vp, grad, rowc, cumt, cumtp, pairs):
    rows = qn.shape[0]
    col = pl.BlockSpec((rows, LANES), lambda p: (0, p))
    fixed = lambda shape: pl.BlockSpec(shape, lambda p: (0, 0))
    wide = jax.ShapeDtypeStruct((rows, pairs * LANES), jnp.float32)
    low = jax.ShapeDtypeStruct((rows, pairs * LANES), jnp.bfloat16)
    shapes = [(rows, LANES), (TABLE, rows), (TABLE, rows + LANES)]
    return pl.pallas_call(
        backward_kernel,
        grid=(pairs,),
        out_shape=[wide, wide, wide, low, low]
        + [jax.ShapeDtypeStruct(shape, jnp.float32) for shape in shapes],
        in_specs=[col] * 6 + [fixed((rows, LANES)), fixed((TABLE, rows)), fixed((TABLE, rows))],
        out_specs=[col] * 5 + [fixed(shape) for shape in shapes],
        scratch_shapes=[pltpu.VMEM((2, rows, LANES), jnp.float32)] * 2,
        name="attend_back",
    )(qn, kn, vb, kp, vp, grad, rowc, cumt, cumtp)


def finish_back(proj, gains, bias, dq, dk, dv, dkr, dvr, dcq, dck, dckr, dog, pairs):
    rows = proj.shape[0]
    at = lambda base: pl.BlockSpec((rows, LANES), lambda p: (0, base + p))
    col = at(0)
    fixed = lambda shape: pl.BlockSpec(shape, lambda p: (0, 0))
    total = (4 * pairs + 1) * LANES
    return pl.pallas_call(
        post_kernel,
        grid=(pairs,),
        out_shape=[
            jax.ShapeDtypeStruct((rows, total), jnp.bfloat16),
            jax.ShapeDtypeStruct((8, LANES), jnp.float32),
            jax.ShapeDtypeStruct((8, LANES), jnp.float32),
        ],
        in_specs=[
            at(0), at(pairs), pl.BlockSpec((rows, LANES), lambda p: (0, 4 * pairs)),
            fixed((1, LANES)), fixed((1, LANES)), fixed((1, LANES)),
            col, col, col, col, col,
            fixed((rows, LANES)), fixed((TABLE, rows)), fixed((TABLE, rows + LANES)), col,
        ],
        out_specs=[fixed((rows, total)), fixed((8, LANES)), fixed((8, LANES))],
        scratch_shapes=[pltpu.VMEM((LANES, rows), jnp.float32)],
        name="finish_back",
    )(proj, proj, proj, gains[0], gains[1], bias, dq, dk, dv, dkr, dvr, dcq, dck, dckr, dog)


def shards(
    mesh,
    tokens,
    cotangent,
    w_qkv,
    w_forget,
    w_ogate,
    w_out,
    w_gu,
    w_down,
    norm_attn,
    norm_ffn,
    query_gain,
    key_gain,
    forget_bias,
    ogate_bias,
):
    inputs = tokens[0].astype(jnp.float32)
    grad_top = cotangent[0].astype(jnp.float32)
    grad_low = cotangent[0]
    rows, width = inputs.shape
    heads = forget_bias.shape[0]
    pairs = width // LANES
    hidden = w_gu.shape[1] // 2
    groups = mesh.shape["dp"] * mesh.shape["ctx"]
    levels = mesh.shape["fsdp"]
    cut = lambda shard: shard.reshape(groups, shard.shape[0] // groups, shard.shape[1])
    forget_wide = jnp.pad(w_forget, ((0, 0), (0, LANES - heads)))
    first = cut(jnp.concatenate([w_qkv, w_ogate, forget_wide], axis=1))
    second = cut(jnp.concatenate([w_out, w_gu], axis=1))
    (proj_full,) = gather_weights(mesh, (first,), 1)
    proj_full = proj_full.reshape(-1, proj_full.shape[2])

    factor_one = rms_factor(inputs)
    act_one = (inputs * factor_one * norm_attn).astype(jnp.bfloat16)
    proj = jnp.dot(act_one, proj_full, preferred_element_type=jnp.float32)
    gains = tuple(jnp.concatenate([gain, gain])[None] for gain in (query_gain, key_gain))
    bias = jnp.pad(forget_bias, (0, LANES - heads))[None]
    qn, kn, vb, cum, cumt = prepare(proj, gains, bias, pairs)
    kp, vp, cumtp = (lax.ppermute(part, "ctx", [(0, 1)]) for part in (kn, vb, cumt))
    second, third, kn, vb, cumt = lax.optimization_barrier((second, cut(w_down), kn, vb, cumt))
    mid_full, down_full = gather_weights(mesh, (second, third), 2)
    kp, vp, cumtp, mid_full, down_full = lax.optimization_barrier((kp, vp, cumtp, mid_full, down_full))
    mid_full, down_full = (full.reshape(-1, full.shape[2]) for full in (mid_full, down_full))
    out_full, gu_full = mid_full[:, :width], mid_full[:, width:]
    attn, rowc = attend(qn, kn, vb, kp, vp, cum, cumt, cumtp, pairs)
    ogate = jax.nn.sigmoid(proj[:, 3 * width : 4 * width] + ogate_bias)
    gated = (attn * ogate).astype(jnp.bfloat16)
    middle = inputs + jnp.dot(gated, out_full, preferred_element_type=jnp.float32)
    factor_two = rms_factor(middle)
    act_two = (middle * factor_two * norm_ffn).astype(jnp.bfloat16)
    gate_up = jnp.dot(act_two, gu_full, preferred_element_type=jnp.float32)
    gate_part = gate_up[:, :hidden]
    up_part = gate_up[:, hidden:]
    hidden_low = (jax.nn.silu(gate_part) * up_part).astype(jnp.bfloat16)
    result = middle + jnp.dot(hidden_low, down_full, preferred_element_type=jnp.float32)

    grad_down = inner_rows(hidden_low, grad_low).astype(jnp.bfloat16)
    grad_hidden = times_trans(grad_low, down_full)
    sigma = jax.nn.sigmoid(gate_part)
    grad_gu_low = jnp.concatenate(
        [
            grad_hidden * up_part * sigma * (1.0 + gate_part * (1.0 - sigma)),
            grad_hidden * (gate_part * sigma),
        ],
        axis=1,
    ).astype(jnp.bfloat16)
    grad_gu = inner_rows(act_two, grad_gu_low).astype(jnp.bfloat16)
    grad_act_two = times_trans(grad_gu_low, gu_full)
    grad_norm_ffn = jnp.sum(grad_act_two * middle * factor_two, axis=0)
    grad_middle = grad_top + rms_back(middle, factor_two, grad_act_two, norm_ffn)
    middle_low = grad_middle.astype(jnp.bfloat16)
    grad_out = inner_rows(gated, middle_low).astype(jnp.bfloat16)
    grad_gated = times_trans(middle_low, out_full)
    grad_attn_low = (grad_gated * ogate).astype(jnp.bfloat16)
    grad_ogate_pre = grad_gated * attn * ogate * (1.0 - ogate)
    grad_ogate_bias = jnp.sum(grad_ogate_pre, axis=0)
    ogate_low = grad_ogate_pre.astype(jnp.bfloat16)

    dq, dk, dv, dkp, dvp, dcq, dck, dckp = attend_back(
        qn, kn, vb, kp, vp, grad_attn_low, rowc, cumt, cumtp, pairs
    )
    dkr, dvr, dckr = (lax.ppermute(part, "ctx", [(1, 0)]) for part in (dkp, dvp, dckp))
    early = lax.optimization_barrier(
        (grad_out, grad_gu, grad_down, grad_norm_ffn, grad_ogate_bias, dq, dkp, dvp, dckp)
    )
    dq = early[5]
    (own_out, own_gu, own_down), (sum_norm_ffn, sum_ogate_bias) = reduce_all(
        mesh, early[:3], early[3:5], 3
    )
    dkr, dvr, dckr, own_out, own_gu, own_down = lax.optimization_barrier(
        (dkr, dvr, dckr, own_out, own_gu, own_down)
    )
    proj_low, gain_sums, bias_sums = finish_back(
        proj, gains, bias, dq, dk, dv, dkr, dvr, dcq, dck, dckr, ogate_low, pairs
    )
    grad_proj = inner_rows(act_one, proj_low)
    grad_act_one = times_trans(proj_low, proj_full)
    grad_norm_attn = jnp.sum(grad_act_one * inputs * factor_one, axis=0)
    grad_inputs = grad_middle + rms_back(inputs, factor_one, grad_act_one, norm_attn)

    small = (
        grad_norm_attn,
        gain_sums[0, :HALF] + gain_sums[0, HALF:],
        gain_sums[1, :HALF] + gain_sums[1, HALF:],
        bias_sums[0, :heads],
    )
    (own_proj,), small = reduce_all(mesh, (grad_proj,), small, 4)
    return (
        result[None],
        grad_inputs[None],
        own_proj[:, : 3 * width],
        own_proj[:, 4 * width : 4 * width + heads],
        own_proj[:, 3 * width : 4 * width],
        own_out,
        own_gu,
        own_down,
        small[0],
        sum_norm_ffn,
        small[1],
        small[2],
        small[3],
        sum_ogate_bias,
    )


def solution(mesh):
    block = P(("dp", "fsdp"), "ctx", None)
    rows = P("fsdp", None)
    return jax.shard_map(
        functools.partial(shards, mesh),
        mesh=mesh,
        in_specs=(block, block) + (rows,) * 6 + (P(),) * 6,
        out_specs=(block, block) + (rows,) * 6 + (P(),) * 6,
        check_vma=False,
    )
```

```python
import functools

import jax
import jax.numpy as jnp
from jax import lax
from jax.experimental import pallas as pl
from jax.experimental.pallas import tpu as pltpu
from jax.sharding import PartitionSpec as P

EPS = 1e-06
NEG_FILL = -1e30
LANES = 128
HALF = 64
TABLE = 16


def rms_factor(values):
    return lax.rsqrt(jnp.mean(values * values, axis=-1, keepdims=True) + EPS)


def rms_back(values, factor, grad_normed, gain):
    scaled = grad_normed * gain
    inner = jnp.mean(scaled * values, axis=-1, keepdims=True)
    return factor * scaled - factor * factor * factor * values * inner


def inner_rows(left, right):
    return lax.dot_general(
        left, right, (((0,), (0,)), ((), ())), preferred_element_type=jnp.float32
    )


def times_trans(left, right):
    return lax.dot_general(
        left, right, (((1,), (1,)), ((), ())), preferred_element_type=jnp.float32
    )


def lane_ids(rows):
    return lax.broadcasted_iota(jnp.int32, (rows, LANES), 1)


def head_half(pair_block, half):
    lanes = lane_ids(pair_block.shape[0])
    inside = (lanes < HALF) if half == 0 else (lanes >= HALF)
    return jnp.where(inside, pair_block, jnp.zeros_like(pair_block))


def both_halves(low, high):
    return jnp.where(lane_ids(low.shape[0]) < HALF, low, high)


def half_sums(values):
    lanes = lane_ids(values.shape[0])
    low = jnp.sum(jnp.where(lanes < HALF, values, 0.0), axis=1, keepdims=True)
    high = jnp.sum(jnp.where(lanes >= HALF, values, 0.0), axis=1, keepdims=True)
    return jnp.where(lanes < HALF, low, high)


def head_column(table, head):
    return jnp.sum(jnp.where(lane_ids(table.shape[0]) == head, table, 0.0), axis=1, keepdims=True)


def running_sum(values, reverse):
    rows = values.shape[0]
    at = lax.broadcasted_iota(jnp.int32, values.shape, 0)
    step = 1
    while step < rows:
        if reverse:
            moved = pltpu.roll(values, rows - step, 0)
            values = values + jnp.where(at < rows - step, moved, 0.0)
        else:
            moved = pltpu.roll(values, step, 0)
            values = values + jnp.where(at >= step, moved, 0.0)
        step *= 2
    return values


def log_sigmoid(values):
    return jnp.minimum(values, 0.0) - jnp.log(1.0 + jnp.exp(-jnp.abs(values)))


def prep_kernel(q_ref, k_ref, v_ref, f_ref, gq_ref, gk_ref, bias_ref, qn_ref, kn_ref, vb_ref, cum_ref, cumt_ref):
    query = q_ref[...]
    factor = lax.rsqrt(half_sums(query * query) * (1.0 / HALF) + EPS)
    low = (query * factor * gq_ref[...]).astype(jnp.bfloat16)
    qn_ref[...] = (low.astype(jnp.float32) * HALF ** (-0.5)).astype(jnp.bfloat16)
    keys = k_ref[...]
    factor = lax.rsqrt(half_sums(keys * keys) * (1.0 / HALF) + EPS)
    kn_ref[...] = (keys * factor * gk_ref[...]).astype(jnp.bfloat16)
    vb_ref[...] = v_ref[...].astype(jnp.bfloat16)

    @pl.when(pl.program_id(0) == 0)
    def _():
        cum = running_sum(log_sigmoid(f_ref[...] + bias_ref[...]), False)
        cum_ref[...] = cum
        cumt_ref[...] = cum.T[: cumt_ref.shape[0]]


def weigh(q_half, k_block, row_term, col_term, masked):
    scores = times_trans(q_half, k_block) + row_term - col_term
    if masked:
        rows = lax.broadcasted_iota(jnp.int32, scores.shape, 0)
        cols = lax.broadcasted_iota(jnp.int32, scores.shape, 1)
        scores = jnp.where(cols <= rows, scores, NEG_FILL)
    return jnp.exp(scores)


def forward_kernel(q_ref, k_ref, v_ref, kp_ref, vp_ref, cum_ref, cumt_ref, cumtp_ref, o_ref, rowc_ref, acc, tot):
    pair = pl.program_id(0)
    rows = q_ref.shape[0]
    block = rows // 2
    past = lax.axis_index("ctx") > 0

    @pl.when(pair == 0)
    def _():
        rowc_ref[...] = jnp.zeros_like(rowc_ref)

    for half in range(2):
        head = 2 * pair + half
        col = cumt_ref[pl.ds(head, 1), :]
        for qb in range(2):
            span = slice(qb * block, (qb + 1) * block)
            row = head_column(cum_ref[span, :], head)
            q_half = head_half(q_ref[span, :], half)
            weights = weigh(q_half, k_ref[span, :], row, col[:, span], True)
            total = jnp.sum(weights, axis=1, keepdims=True)
            attended = jnp.dot(
                weights.astype(jnp.bfloat16), v_ref[span, :], preferred_element_type=jnp.float32
            )
            if qb == 1:
                weights = weigh(q_half, k_ref[:block, :], row, col[:, :block], False)
                total = total + jnp.sum(weights, axis=1, keepdims=True)
                attended = attended + jnp.dot(
                    weights.astype(jnp.bfloat16), v_ref[:block, :], preferred_element_type=jnp.float32
                )
            acc[half, span, :] = attended
            tot[half, span, :] = total

    @pl.when(past)
    def _():
        for half in range(2):
            head = 2 * pair + half
            col = cumtp_ref[pl.ds(head, 1), :]
            col = col - col[:, rows - 1 : rows]
            for qb in range(2):
                span = slice(qb * block, (qb + 1) * block)
                row = head_column(cum_ref[span, :], head)
                q_half = head_half(q_ref[span, :], half)
                weights = weigh(q_half, kp_ref[...], row, col, False)
                acc[half, span, :] += jnp.dot(
                    weights.astype(jnp.bfloat16), vp_ref[...], preferred_element_type=jnp.float32
                )
                tot[half, span, :] += jnp.sum(weights, axis=1, keepdims=True)

    o_ref[...] = both_halves(acc[0] / tot[0], acc[1] / tot[1])
    lanes = lane_ids(rows)
    table = rowc_ref[...]
    for half in range(2):
        head = 2 * pair + half
        row = head_column(cum_ref[...], head) - jnp.log(tot[half])
        table = jnp.where(lanes == head, row, table)
    rowc_ref[...] = table


def backward_kernel(
    q_ref, k_ref, v_ref, kp_ref, vp_ref, do_ref, rowc_ref, cumt_ref, cumtp_ref,
    dq_ref, dk_ref, dv_ref, dkp_ref, dvp_ref, dcq_ref, dck_ref, dckp_ref, kacc, vacc,
):
    pair = pl.program_id(0)
    rows = q_ref.shape[0]
    block = rows // 2
    rank = lax.axis_index("ctx")

    @pl.when(pair == 0)
    def _():
        dcq_ref[...] = jnp.zeros_like(dcq_ref)
        dck_ref[...] = jnp.zeros_like(dck_ref)
        dckp_ref[...] = jnp.zeros_like(dckp_ref)

    def run(with_past):
        kacc[...] = jnp.zeros_like(kacc)
        vacc[...] = jnp.zeros_like(vacc)
        for half in range(2):
            head = 2 * pair + half
            col = cumt_ref[pl.ds(head, 1), :]
            if with_past:
                colp = cumtp_ref[pl.ds(head, 1), :]
                colp = colp - colp[:, rows - 1 : rows]
            down_total = jnp.zeros((1, 1), jnp.float32)
            for qb in range(2):
                span = slice(qb * block, (qb + 1) * block)
                row = head_column(rowc_ref[span, :], head)
                q_half = head_half(q_ref[span, :], half)
                do_half = head_half(do_ref[span, :], half)
                pieces = [(k_ref, v_ref, span, col[:, span], True, 0)]
                if qb == 1:
                    pieces.append((k_ref, v_ref, slice(0, block), col[:, :block], False, 0))
                if with_past:
                    for kb in range(2):
                        part = slice(kb * block, (kb + 1) * block)
                        pieces.append((kp_ref, vp_ref, part, colp[:, part], False, 1))
                probs, grads = [], []
                delta = jnp.zeros((block, 1), jnp.float32)
                for keys, values, part, cols, masked, where in pieces:
                    prob = weigh(q_half, keys[part, :], row, cols, masked)
                    grad = times_trans(do_half, values[part, :])
                    delta = delta + jnp.sum(prob * grad, axis=1, keepdims=True)
                    vacc[where, part, :] += inner_rows(prob.astype(jnp.bfloat16), do_half)
                    probs.append(prob)
                    grads.append(grad)
                query_grad = jnp.zeros((block, LANES), jnp.float32)
                row_sum = jnp.zeros((block, 1), jnp.float32)
                for (keys, values, part, cols, masked, where), prob, grad in zip(pieces, probs, grads):
                    score_grad = prob * (grad - delta)
                    low = score_grad.astype(jnp.bfloat16)
                    query_grad = query_grad + jnp.dot(
                        low, keys[part, :], preferred_element_type=jnp.float32
                    )
                    kacc[where, part, :] += inner_rows(low, q_half)
                    row_sum = row_sum + jnp.sum(score_grad, axis=1, keepdims=True)
                    col_sum = jnp.sum(score_grad, axis=0, keepdims=True)
                    target = dckp_ref if where else dck_ref
                    target[pl.ds(head, 1), part] += -col_sum
                    if not where:
                        down_total = down_total - jnp.sum(col_sum, axis=1, keepdims=True)
                query_grad = query_grad * HALF ** (-0.5)
                if half == 0:
                    dq_ref[span, :] = query_grad
                else:
                    dq_ref[span, :] = both_halves(dq_ref[span, :], query_grad)
                dcq_ref[span, :] = jnp.where(lane_ids(block) == head, row_sum, dcq_ref[span, :])
                down_total = down_total + jnp.sum(row_sum, axis=0, keepdims=True)
            table = dckp_ref[:, rows:]
            at = lax.broadcasted_iota(jnp.int32, table.shape, 0)
            dckp_ref[:, rows:] = jnp.where(at == head, down_total, table)
        dk_ref[...] = kacc[0]
        dv_ref[...] = vacc[0]
        dkp_ref[...] = kacc[1].astype(jnp.bfloat16)
        dvp_ref[...] = vacc[1].astype(jnp.bfloat16)

    @pl.when(rank == 0)
    def _():
        run(False)

    @pl.when(rank > 0)
    def _():
        run(True)


def rms_back_pair(values, grad, gain):
    factor = lax.rsqrt(half_sums(values * values) * (1.0 / HALF) + EPS)
    scaled = grad * gain
    inner = half_sums(scaled * values) * (1.0 / HALF)
    gain_grad = jnp.sum(grad * values * factor, axis=0, keepdims=True)
    return factor * scaled - factor * factor * factor * values * inner, gain_grad


def post_kernel(
    q_ref, k_ref, f_ref, gq_ref, gk_ref, bias_ref, dq_ref, dk_ref, dv_ref, dkr_ref, dvr_ref,
    dcq_ref, dck_ref, dckr_ref, dog_ref, out_ref, gains_ref, dbias_ref, flip,
):
    pair = pl.program_id(0)
    pairs = pl.num_programs(0)
    rows = q_ref.shape[0]
    width = pairs * LANES

    def place(base):
        return pl.ds(pl.multiple_of(base + pair * LANES, LANES), LANES)

    grad, query_gain = rms_back_pair(q_ref[...], dq_ref[...], gq_ref[...])
    out_ref[:, place(0)] = grad.astype(jnp.bfloat16)
    key_grad = dk_ref[...] + dkr_ref[...].astype(jnp.float32)
    grad, key_gain = rms_back_pair(k_ref[...], key_grad, gk_ref[...])
    out_ref[:, place(width)] = grad.astype(jnp.bfloat16)
    out_ref[:, place(2 * width)] = (dv_ref[...] + dvr_ref[...].astype(jnp.float32)).astype(jnp.bfloat16)
    out_ref[:, place(3 * width)] = dog_ref[...]

    @pl.when(pair == 0)
    def _():
        gains_ref[...] = jnp.zeros_like(gains_ref)
        count = dck_ref.shape[0]
        flip[...] = jnp.zeros_like(flip)
        flip[:count, :] = dck_ref[...] + dckr_ref[:, :rows]
        cum_grad = dcq_ref[...] + flip[...].T
        flip[...] = jnp.zeros_like(flip)
        flip[:count, :LANES] = dckr_ref[:, rows:]
        later = flip[:, :LANES].T[:1, :]
        log_grad = running_sum(cum_grad, True) + later
        gate = f_ref[...] + bias_ref[...]
        gate_grad = log_grad * jax.nn.sigmoid(-gate)
        dbias_ref[...] = jnp.broadcast_to(jnp.sum(gate_grad, axis=0, keepdims=True), dbias_ref.shape)
        out_ref[:, 4 * width :] = gate_grad.astype(jnp.bfloat16)

    gains_ref[0:1, :] += query_gain
    gains_ref[1:2, :] += key_gain


def gather_weights(mesh, pieces, call, parts):
    groups, levels, halves = mesh.shape["dp"] * mesh.shape["ctx"], mesh.shape["fsdp"], mesh.shape["ctx"]
    count = len(pieces)
    chips = groups // 2

    def body(*refs):
        ins, outs = refs[:count], refs[count : 2 * count]
        keep_sem, z_sem, peer_sem, core_sem, got_sem, far_sem, half_sem = refs[2 * count :]
        dp, z, y = lax.axis_index("dp"), lax.axis_index("fsdp"), lax.axis_index("ctx")
        core = dp % 2
        mine = dp * halves + y
        chip = (dp // 2) * halves + y

        def group_of(other_chip, other_core):
            return ((other_chip // halves) * 2 + other_core) * halves + other_chip % halves

        def place(group, level):
            return {"dp": group // halves, "fsdp": level, "ctx": group % halves}

        barrier = pltpu.get_barrier_semaphore()

        def greet(group, level):
            pl.semaphore_signal(
                barrier, inc=1, device_id=place(group, level), device_id_type=pl.DeviceIdType.MESH
            )

        sibling = group_of(chip, 1 - core)
        greet(sibling, z)
        for hop in range(1, chips):
            greet(group_of((chip ^ hop), core), z)

        @pl.when(z > 0)
        def _():
            greet(mine, z - 1)

        @pl.when(z < levels - 1)
        def _():
            greet(mine, z + 1)

        ends = jnp.minimum(z, 1) + jnp.minimum(levels - 1 - z, 1)
        pl.semaphore_wait(barrier, chips + ends)

        def copy(a, level, group, to_group, to_level, sem, own=False):
            slot = level * groups + group
            return pltpu.make_async_remote_copy(
                src_ref=ins[a].at[group] if own else outs[a].at[slot],
                dst_ref=outs[a].at[slot],
                send_sem=sem,
                recv_sem=got_sem.at[a, slot],
                device_id=place(to_group, to_level),
                device_id_type=pl.DeviceIdType.MESH,
            )

        def z_copy(a, level, side, own=False):
            return copy(a, level, mine, mine, z + (1 if side else -1), z_sem.at[a, level, side], own)

        def peer_copy(a, level, hop):
            return copy(a, level, mine, group_of((chip ^ hop), core), z, peer_sem.at[a, level, hop])

        def core_copy(a, level, hop):
            return copy(a, level, group_of((chip ^ hop), core), sibling, z, core_sem.at[a, level, hop])

        def far_copy(a, level, way):
            width = outs[a].shape[2]
            cut = (width // (parts * LANES)) * LANES if parts else 0
            cols = pl.ds(cut, width - cut) if way else pl.ds(0, cut)
            slot = level * groups + group_of(chip ^ (1 if way else 2), core)
            return pltpu.make_async_remote_copy(
                src_ref=outs[a].at[slot, :, cols],
                dst_ref=outs[a].at[slot, :, cols],
                send_sem=far_sem.at[a, level, way],
                recv_sem=half_sem.at[a, level, way],
                device_id=place(group_of(chip ^ (2 if way else 1), core), z),
                device_id_type=pl.DeviceIdType.MESH,
            )

        def far_arrived(a, level, way):
            width = outs[a].shape[2]
            cut = (width // (parts * LANES)) * LANES if parts else 0
            cols = pl.ds(cut, width - cut) if way else pl.ds(0, cut)
            slot = level * groups + group_of(chip ^ 3, core)
            pltpu.make_async_remote_copy(
                src_ref=outs[a].at[slot, :, cols],
                dst_ref=outs[a].at[slot, :, cols],
                send_sem=far_sem.at[a, level, way],
                recv_sem=half_sem.at[a, level, way],
                device_id=place(sibling, z),
                device_id_type=pl.DeviceIdType.MESH,
            ).wait_recv()

        def arrived(a, level, group):
            copy(a, level, group, sibling, z, core_sem.at[a, level, 0]).wait_recv()

        def kept(a):
            return pltpu.make_async_copy(ins[a], outs[a].at[pl.ds(z * groups, groups)], keep_sem.at[a])

        relay = chips == 4
        direct = range(1, 3 if relay else chips)
        ways = range(2) if parts else range(1, 2)

        def edges(action):
            for a in range(count):

                @pl.when(z < levels - 1)
                def _():
                    action(z_copy(a, z, 1, True))

                @pl.when(z > 0)
                def _():
                    action(z_copy(a, z, 0, True))

        edges(lambda item: item.start())
        for a in range(count):
            kept(a).start()

        def near(a, level, side, last):
            arrived(a, level, mine)

            @pl.when(jnp.logical_not(last))
            def _():
                z_copy(a, level, side).start()

            for hop in direct:
                peer_copy(a, level, hop).start()
            core_copy(a, level, 0).start()

        def spread(a, level):
            for hop in direct:
                arrived(a, level, group_of(chip ^ hop, core))
                if relay and 2 - hop in ways:
                    far_copy(a, level, 2 - hop).start()
                core_copy(a, level, hop).start()

        def close(a, level):
            if relay:
                for way in ways:
                    far_arrived(a, level, way)
                core_copy(a, level, 3).start()

        units = [(a, step) for a in range(count) for step in range(1, levels)]

        def sides(index, action):
            if 0 <= index < len(units):
                a, step = units[index]

                @pl.when(z - step >= 0)
                def _():
                    action(a, z - step, 1, z == levels - 1)

                @pl.when(z + step < levels)
                def _():
                    action(a, z + step, 0, z == 0)

        for index in range(len(units) + 2):
            sides(index, near)
            sides(index - 1, lambda a, level, side, last: spread(a, level))
            sides(index - 2, lambda a, level, side, last: close(a, level))

        def others(action):
            for a in range(count):
                for step in range(1, levels):
                    level = (z + step) % levels
                    action(a, level)

        def finish(a, level):
            for hop in range(chips):
                arrived(a, level, group_of(chip ^ hop, 1 - core))
            for hop in range(chips):
                core_copy(a, level, hop).wait_send()
            for hop in direct:
                peer_copy(a, level, hop).wait_send()
            if relay:
                for way in ways:
                    far_copy(a, level, way).wait_send()

        others(finish)
        edges(lambda item: item.wait_send())
        for a in range(count):
            kept(a).wait()
            for step in range(1, levels):

                @pl.when(jnp.logical_and(z - step >= 0, z < levels - 1))
                def _():
                    z_copy(a, z - step, 1).wait_send()

                @pl.when(jnp.logical_and(z + step < levels, z > 0))
                def _():
                    z_copy(a, z + step, 0).wait_send()

    dma = pltpu.SemaphoreType.DMA
    return pl.pallas_call(
        body,
        out_shape=[
            jax.ShapeDtypeStruct((levels * groups,) + piece.shape[1:], piece.dtype) for piece in pieces
        ],
        in_specs=[pl.BlockSpec(memory_space=pltpu.VMEM)] * count,
        out_specs=[pl.BlockSpec(memory_space=pl.ANY)] * count,
        scratch_shapes=[
            dma((count,)),
            dma((count, levels, 2)),
            dma((count, levels, chips)),
            dma((count, levels, chips)),
            dma((count, levels * groups)),
            dma((count, levels, 2)),
            dma((count, levels, 2)),
        ],
        compiler_params=pltpu.CompilerParams(collective_id=call, has_side_effects=True),
        cost_estimate=pl.CostEstimate(
            flops=0, bytes_accessed=20 * levels * sum(p.size for p in pieces), transcendentals=0
        ),
        name="gather_weights",
    )(*pieces)


def reduce_kernel(mesh, grads, small, call, mixed):
    halves, levels = mesh.shape["ctx"], mesh.shape["fsdp"]
    groups = mesh.shape["dp"] * halves
    chips = groups // 2
    count = len(grads)
    wide = jnp.float32

    def body(*refs):
        ins, small_in = refs[:count], refs[count]
        outs, small_out = refs[count + 1 : 2 * count + 1], refs[2 * count + 1]
        rest = refs[2 * count + 2 :]
        pair_buf, quad_buf, z_buf = rest[:count], rest[count : 2 * count], rest[2 * count : 3 * count]
        s_pair, s_quad, s_z, sems = rest[3 * count : 3 * count + 3] + (rest[3 * count + 3 :],)
        pair_s, pair_r, quad_s, quad_r, lev_s, lev_r, peer_s, core_s, got_r = sems[:9]
        sp_s, sp_r, sq_s, sq_r, sz_s, sz_r = sems[9:]
        dp, z, y = lax.axis_index("dp"), lax.axis_index("fsdp"), lax.axis_index("ctx")
        core = dp % 2
        mine = dp * halves + y
        chip = (dp // 2) * halves + y

        def group_of(other_chip, other_core):
            return ((other_chip // halves) * 2 + other_core) * halves + other_chip % halves

        def place(group, level):
            return {"dp": group // halves, "fsdp": level, "ctx": group % halves}

        sibling = group_of(chip, 1 - core)

        def peer(hop):
            return group_of((chip ^ hop), core)

        barrier = pltpu.get_barrier_semaphore()

        def greet(group, level):
            pl.semaphore_signal(
                barrier, inc=1, device_id=place(group, level), device_id_type=pl.DeviceIdType.MESH
            )

        greet(sibling, z)
        for hop in range(1, chips):
            greet(peer(hop), z)
        for step in range(1, levels):
            greet(mine, (z + step) % levels)
        pl.semaphore_wait(barrier, chips + levels - 1)

        def remote(src, dst, send, recv, group, level):
            return pltpu.make_async_remote_copy(
                src_ref=src, dst_ref=dst, send_sem=send, recv_sem=recv,
                device_id=place(group, level), device_id_type=pl.DeviceIdType.MESH,
            )

        def pair_copy(a, step, other_chip):
            level = (z + step) % levels
            return remote(
                ins[a].at[level * groups + group_of(other_chip, 1 - core)],
                pair_buf[a].at[step, other_chip],
                pair_s.at[a, step, other_chip], pair_r.at[a, step, other_chip], sibling, z,
            )

        halving = chips == 4

        def first_hop(step):
            return 1 if mixed and step % 2 else 2

        def quad_copy(a, step, hop):
            near, slot, target = first_hop(step), hop - 1, hop
            if halving:
                slot = {near: 0, 3: 1, 3 - near: 2}[hop]
                target = near if hop == 3 else hop
            return remote(
                pair_buf[a].at[step, chip ^ hop],
                quad_buf[a].at[step, slot],
                quad_s.at[a, step, hop], quad_r.at[a, step, hop], peer(target), z,
            )

        def level_copy(a, step):
            return remote(
                pair_buf[a].at[step, chip],
                z_buf[a].at[step - 1],
                lev_s.at[a, step], lev_r.at[a, step], mine, (z + step) % levels,
            )

        def peer_copy(a, hop):
            return remote(
                outs[a].at[mine], outs[a].at[mine], peer_s.at[a, hop], got_r.at[a, mine], peer(hop), z
            )

        def core_copy(a, hop):
            group = peer(hop)
            return remote(
                outs[a].at[group], outs[a].at[group], core_s.at[a, hop], got_r.at[a, group], sibling, z
            )

        def arrived(a, group):
            remote(
                outs[a].at[group], outs[a].at[group], core_s.at[a, 0], got_r.at[a, group], sibling, z
            ).wait_recv()

        small_pair = remote(small_in, s_pair, sp_s, sp_r, sibling, z)

        def small_quad(hop):
            return remote(
                s_quad.at[chip], s_quad.at[chip], sq_s.at[hop], sq_r.at[chip], peer(hop), z
            )

        def small_level(step):
            return remote(
                s_z.at[z], s_z.at[z], sz_s.at[step], sz_r.at[z], mine, (z + step) % levels
            )

        small_pair.start()
        steps = list(range(1, levels)) + [0]
        units = [(a, step) for a in range(count) for step in steps]
        for a, step in units:
            for other in range(chips):
                pair_copy(a, step, other).start()

        small_pair.wait_recv()
        s_quad[chip] = small_in[...] + s_pair[...]

        def pair_sum(a, step):
            level = (z + step) % levels

            def one(other, carry):
                pair_copy(a, step, other).wait_recv()
                own = ins[a][level * groups + group_of(other, core)].astype(wide)
                total = own + pair_buf[a][step, other].astype(wide)
                pair_buf[a][step, other] = total.astype(jnp.bfloat16)
                return carry

            lax.fori_loop(0, chips, one, 0)

        def quad_sum(a, step):
            for hop in range(1, chips):
                quad_copy(a, step, hop).wait_recv()
            total = pair_buf[a][step, chip].astype(wide)
            for hop in range(1, chips):
                total = total + quad_buf[a][step, hop - 1].astype(wide)
            pair_buf[a][step, chip] = total.astype(jnp.bfloat16)

        def level_sum(a):
            for step in range(1, levels):
                level_copy(a, step).wait_recv()
            total = pair_buf[a][0, chip].astype(wide)
            for step in range(1, levels):
                total = total + z_buf[a][step - 1].astype(wide)
            outs[a][mine] = total.astype(jnp.bfloat16)

        def half_sum(a, step):
            other = 3 - first_hop(step)
            quad_copy(a, step, 3).wait_recv()
            total = pair_buf[a][step, chip ^ other].astype(wide) + quad_buf[a][step, 1].astype(wide)
            pair_buf[a][step, chip ^ other] = total.astype(jnp.bfloat16)

        def full_sum(a, step):
            near = first_hop(step)
            quad_copy(a, step, near).wait_recv()
            quad_copy(a, step, 3 - near).wait_recv()
            total = pair_buf[a][step, chip].astype(wide) + quad_buf[a][step, 0].astype(wide)
            total = total + quad_buf[a][step, 2].astype(wide)
            pair_buf[a][step, chip] = total.astype(jnp.bfloat16)

        wait_half, lag = (2, 4) if halving else (0, 2)
        for index in range(len(units) + lag):
            now = units[index] if index < len(units) else None
            late = units[index - lag] if index >= lag else None
            middle = None
            if halving and 0 <= index - wait_half < len(units):
                middle = units[index - wait_half]
            if now:
                pair_sum(*now)
            if middle:
                half_sum(*middle)
            if late:
                (full_sum if halving else quad_sum)(*late)
            if index == 0:
                for hop in range(1, chips):
                    small_quad(hop).start()
            if now:
                for hop in range(1, chips):
                    if not halving or hop != 3 - first_hop(now[1]):
                        quad_copy(*now, hop).start()
            if middle:
                quad_copy(*middle, 3 - first_hop(middle[1])).start()
            if late and late[1] > 0:
                level_copy(*late).start()

        def small_wait_quad(other):
            remote(
                s_quad.at[other], s_quad.at[other], sq_s.at[0], sq_r.at[other], sibling, z
            ).wait_recv()

        for hop in range(1, chips):
            small_wait_quad((chip ^ hop))
        total = s_quad[0]
        for other in range(1, chips):
            total = total + s_quad[other]
        s_z[z] = total
        for a in range(count):
            level_sum(a)
            if a == 0:
                for step in range(1, levels):
                    small_level(step).start()
            if a > 0:
                for hop in range(1, chips):
                    peer_copy(a - 1, hop).start()
                core_copy(a - 1, 0).start()

        for step in range(1, levels):
            other = (z + step) % levels
            remote(s_z.at[other], s_z.at[other], sz_s.at[0], sz_r.at[other], sibling, z).wait_recv()
        for hop in range(1, chips):
            peer_copy(count - 1, hop).start()
        core_copy(count - 1, 0).start()
        total = s_z[0]
        for other in range(1, levels):
            total = total + s_z[other]
        small_out[...] = total

        for a in range(count):
            for hop in range(1, chips):
                arrived(a, peer(hop))
                core_copy(a, hop).start()
        for a in range(count):
            for hop in range(chips):
                arrived(a, group_of((chip ^ hop), 1 - core))

        small_pair.wait_send()
        for hop in range(1, chips):
            small_quad(hop).wait_send()
        for step in range(1, levels):
            small_level(step).wait_send()
        for a, step in units:
            for other in range(chips):
                pair_copy(a, step, other).wait_send()
            for hop in range(1, chips):
                quad_copy(a, step, hop).wait_send()
            if step > 0:
                level_copy(a, step).wait_send()
        for a in range(count):
            for hop in range(1, chips):
                peer_copy(a, hop).wait_send()
            for hop in range(chips):
                core_copy(a, hop).wait_send()

    dma = pltpu.SemaphoreType.DMA
    shapes = [grad.shape[1:] for grad in grads]
    low = jnp.bfloat16
    vmem = pl.BlockSpec(memory_space=pltpu.VMEM)
    return pl.pallas_call(
        body,
        out_shape=[jax.ShapeDtypeStruct((groups,) + shape, low) for shape in shapes]
        + [jax.ShapeDtypeStruct(small.shape, small.dtype)],
        in_specs=[vmem] * (count + 1),
        out_specs=[vmem] * (count + 1),
        scratch_shapes=[pltpu.VMEM((levels, chips) + shape, low) for shape in shapes]
        + [pltpu.VMEM((levels, chips - 1) + shape, low) for shape in shapes]
        + [pltpu.VMEM((levels - 1,) + shape, low) for shape in shapes]
        + [
            pltpu.VMEM(small.shape, small.dtype),
            pltpu.VMEM((chips,) + small.shape, small.dtype),
            pltpu.VMEM((levels,) + small.shape, small.dtype),
            dma((count, levels, chips)), dma((count, levels, chips)),
            dma((count, levels, chips)), dma((count, levels, chips)),
            dma((count, levels)), dma((count, levels)),
            dma((count, chips)), dma((count, chips)), dma((count, groups)),
            dma, dma, dma((chips,)), dma((chips,)), dma((levels,)), dma((levels,)),
        ],
        compiler_params=pltpu.CompilerParams(
            collective_id=call, has_side_effects=True, vmem_limit_bytes=60 * 1024 * 1024
        ),
        cost_estimate=pl.CostEstimate(
            flops=0, bytes_accessed=20 * sum(grad.size for grad in grads), transcendentals=0
        ),
        name="reduce_grads",
    )(*grads, small)


def reduce_all(mesh, grads, small, call, mixed):
    pieces = mesh.shape["fsdp"] * mesh.shape["dp"] * mesh.shape["ctx"]
    cut = [
        grad.astype(jnp.bfloat16).reshape(pieces, grad.shape[0] // pieces, grad.shape[1])
        for grad in grads
    ]
    flat = jnp.concatenate(small)
    room = -flat.shape[0] % (8 * LANES)
    flat = jnp.pad(flat, (0, room)).reshape(-1, LANES)
    results = reduce_kernel(mesh, cut, flat, call, mixed)
    owned = [part.reshape(-1, part.shape[2]).astype(jnp.float32) for part in results[:-1]]
    total = results[-1].reshape(-1)
    sums, start = [], 0
    for part in small:
        sums.append(total[start : start + part.shape[0]])
        start += part.shape[0]
    return owned, sums


def prepare(proj, gains, bias, pairs):
    rows = proj.shape[0]
    col = lambda base: pl.BlockSpec((rows, LANES), lambda p: (0, base + p))
    fixed = lambda shape: pl.BlockSpec(shape, lambda p: (0, 0))
    low = jax.ShapeDtypeStruct((rows, pairs * LANES), jnp.bfloat16)
    return pl.pallas_call(
        prep_kernel,
        grid=(pairs,),
        out_shape=[
            low, low, low,
            jax.ShapeDtypeStruct((rows, LANES), jnp.float32),
            jax.ShapeDtypeStruct((TABLE, rows), jnp.float32),
        ],
        in_specs=[
            col(0), col(pairs), col(2 * pairs),
            pl.BlockSpec((rows, LANES), lambda p: (0, 4 * pairs)),
            fixed((1, LANES)), fixed((1, LANES)), fixed((1, LANES)),
        ],
        out_specs=[col(0), col(0), col(0), fixed((rows, LANES)), fixed((TABLE, rows))],
        name="prep",
    )(proj, proj, proj, proj, gains[0], gains[1], bias)


def attend(qn, kn, vb, kp, vp, cum, cumt, cumtp, pairs):
    rows = qn.shape[0]
    col = pl.BlockSpec((rows, LANES), lambda p: (0, p))
    fixed = lambda shape: pl.BlockSpec(shape, lambda p: (0, 0))
    return pl.pallas_call(
        forward_kernel,
        grid=(pairs,),
        out_shape=[
            jax.ShapeDtypeStruct((rows, pairs * LANES), jnp.float32),
            jax.ShapeDtypeStruct((rows, LANES), jnp.float32),
        ],
        in_specs=[col] * 5 + [fixed((rows, LANES)), fixed((TABLE, rows)), fixed((TABLE, rows))],
        out_specs=[col, fixed((rows, LANES))],
        scratch_shapes=[
            pltpu.VMEM((2, rows, LANES), jnp.float32),
            pltpu.VMEM((2, rows, 1), jnp.float32),
        ],
        name="attend",
    )(qn, kn, vb, kp, vp, cum, cumt, cumtp)


def attend_back(qn, kn, vb, kp, vp, grad, rowc, cumt, cumtp, pairs):
    rows = qn.shape[0]
    col = pl.BlockSpec((rows, LANES), lambda p: (0, p))
    fixed = lambda shape: pl.BlockSpec(shape, lambda p: (0, 0))
    wide = jax.ShapeDtypeStruct((rows, pairs * LANES), jnp.float32)
    low = jax.ShapeDtypeStruct((rows, pairs * LANES), jnp.bfloat16)
    shapes = [(rows, LANES), (TABLE, rows), (TABLE, rows + LANES)]
    return pl.pallas_call(
        backward_kernel,
        grid=(pairs,),
        out_shape=[wide, wide, wide, low, low]
        + [jax.ShapeDtypeStruct(shape, jnp.float32) for shape in shapes],
        in_specs=[col] * 6 + [fixed((rows, LANES)), fixed((TABLE, rows)), fixed((TABLE, rows))],
        out_specs=[col] * 5 + [fixed(shape) for shape in shapes],
        scratch_shapes=[pltpu.VMEM((2, rows, LANES), jnp.float32)] * 2,
        name="attend_back",
    )(qn, kn, vb, kp, vp, grad, rowc, cumt, cumtp)


def finish_back(proj, gains, bias, dq, dk, dv, dkr, dvr, dcq, dck, dckr, dog, pairs):
    rows = proj.shape[0]
    at = lambda base: pl.BlockSpec((rows, LANES), lambda p: (0, base + p))
    col = at(0)
    fixed = lambda shape: pl.BlockSpec(shape, lambda p: (0, 0))
    total = (4 * pairs + 1) * LANES
    return pl.pallas_call(
        post_kernel,
        grid=(pairs,),
        out_shape=[
            jax.ShapeDtypeStruct((rows, total), jnp.bfloat16),
            jax.ShapeDtypeStruct((8, LANES), jnp.float32),
            jax.ShapeDtypeStruct((8, LANES), jnp.float32),
        ],
        in_specs=[
            at(0), at(pairs), pl.BlockSpec((rows, LANES), lambda p: (0, 4 * pairs)),
            fixed((1, LANES)), fixed((1, LANES)), fixed((1, LANES)),
            col, col, col, col, col,
            fixed((rows, LANES)), fixed((TABLE, rows)), fixed((TABLE, rows + LANES)), col,
        ],
        out_specs=[fixed((rows, total)), fixed((8, LANES)), fixed((8, LANES))],
        scratch_shapes=[pltpu.VMEM((LANES, rows), jnp.float32)],
        name="finish_back",
    )(proj, proj, proj, gains[0], gains[1], bias, dq, dk, dv, dkr, dvr, dcq, dck, dckr, dog)


def shards(
    mesh,
    tokens,
    cotangent,
    w_qkv,
    w_forget,
    w_ogate,
    w_out,
    w_gu,
    w_down,
    norm_attn,
    norm_ffn,
    query_gain,
    key_gain,
    forget_bias,
    ogate_bias,
):
    inputs = tokens[0].astype(jnp.float32)
    grad_top = cotangent[0].astype(jnp.float32)
    grad_low = cotangent[0]
    rows, width = inputs.shape
    heads = forget_bias.shape[0]
    pairs = width // LANES
    hidden = w_gu.shape[1] // 2
    groups = mesh.shape["dp"] * mesh.shape["ctx"]
    levels = mesh.shape["fsdp"]
    cut = lambda shard: shard.reshape(groups, shard.shape[0] // groups, shard.shape[1])
    forget_wide = jnp.pad(w_forget, ((0, 0), (0, LANES - heads)))
    first = cut(jnp.concatenate([w_qkv, w_ogate, forget_wide], axis=1))
    second = cut(jnp.concatenate([w_out, w_gu], axis=1))
    (proj_full,) = gather_weights(mesh, (first,), 1, 2)
    proj_full = proj_full.reshape(-1, proj_full.shape[2])

    factor_one = rms_factor(inputs)
    act_one = (inputs * factor_one * norm_attn).astype(jnp.bfloat16)
    proj = jnp.dot(act_one, proj_full, preferred_element_type=jnp.float32)
    gains = tuple(jnp.concatenate([gain, gain])[None] for gain in (query_gain, key_gain))
    bias = jnp.pad(forget_bias, (0, LANES - heads))[None]
    qn, kn, vb, cum, cumt = prepare(proj, gains, bias, pairs)
    kp, vp, cumtp = (lax.ppermute(part, "ctx", [(0, 1)]) for part in (kn, vb, cumt))
    second, third, kn, vb, cumt = lax.optimization_barrier((second, cut(w_down), kn, vb, cumt))
    mid_full, down_full = gather_weights(mesh, (second, third), 2, 0)
    kp, vp, cumtp, mid_full, down_full = lax.optimization_barrier((kp, vp, cumtp, mid_full, down_full))
    mid_full, down_full = (full.reshape(-1, full.shape[2]) for full in (mid_full, down_full))
    out_full, gu_full = mid_full[:, :width], mid_full[:, width:]
    attn, rowc = attend(qn, kn, vb, kp, vp, cum, cumt, cumtp, pairs)
    ogate = jax.nn.sigmoid(proj[:, 3 * width : 4 * width] + ogate_bias)
    gated = (attn * ogate).astype(jnp.bfloat16)
    middle = inputs + jnp.dot(gated, out_full, preferred_element_type=jnp.float32)
    factor_two = rms_factor(middle)
    act_two = (middle * factor_two * norm_ffn).astype(jnp.bfloat16)
    gate_up = jnp.dot(act_two, gu_full, preferred_element_type=jnp.float32)
    gate_part = gate_up[:, :hidden]
    up_part = gate_up[:, hidden:]
    hidden_low = (jax.nn.silu(gate_part) * up_part).astype(jnp.bfloat16)
    result = middle + jnp.dot(hidden_low, down_full, preferred_element_type=jnp.float32)

    grad_down = inner_rows(hidden_low, grad_low).astype(jnp.bfloat16)
    grad_hidden = times_trans(grad_low, down_full)
    sigma = jax.nn.sigmoid(gate_part)
    grad_gu_low = jnp.concatenate(
        [
            grad_hidden * up_part * sigma * (1.0 + gate_part * (1.0 - sigma)),
            grad_hidden * (gate_part * sigma),
        ],
        axis=1,
    ).astype(jnp.bfloat16)
    grad_gu = inner_rows(act_two, grad_gu_low).astype(jnp.bfloat16)
    grad_act_two = times_trans(grad_gu_low, gu_full)
    grad_norm_ffn = jnp.sum(grad_act_two * middle * factor_two, axis=0)
    grad_middle = grad_top + rms_back(middle, factor_two, grad_act_two, norm_ffn)
    middle_low = grad_middle.astype(jnp.bfloat16)
    grad_out = inner_rows(gated, middle_low).astype(jnp.bfloat16)
    grad_gated = times_trans(middle_low, out_full)
    grad_attn_low = (grad_gated * ogate).astype(jnp.bfloat16)
    grad_ogate_pre = grad_gated * attn * ogate * (1.0 - ogate)
    grad_ogate_bias = jnp.sum(grad_ogate_pre, axis=0)
    ogate_low = grad_ogate_pre.astype(jnp.bfloat16)

    dq, dk, dv, dkp, dvp, dcq, dck, dckp = attend_back(
        qn, kn, vb, kp, vp, grad_attn_low, rowc, cumt, cumtp, pairs
    )
    dkr, dvr, dckr = (lax.ppermute(part, "ctx", [(1, 0)]) for part in (dkp, dvp, dckp))
    early = lax.optimization_barrier(
        (grad_out, grad_gu, grad_down, grad_norm_ffn, grad_ogate_bias, dq, dkp, dvp, dckp)
    )
    dq = early[5]
    (own_out, own_gu, own_down), (sum_norm_ffn, sum_ogate_bias) = reduce_all(
        mesh, early[:3], early[3:5], 3, False
    )
    dkr, dvr, dckr, own_out, own_gu, own_down = lax.optimization_barrier(
        (dkr, dvr, dckr, own_out, own_gu, own_down)
    )
    proj_low, gain_sums, bias_sums = finish_back(
        proj, gains, bias, dq, dk, dv, dkr, dvr, dcq, dck, dckr, ogate_low, pairs
    )
    grad_proj = inner_rows(act_one, proj_low)
    grad_act_one = times_trans(proj_low, proj_full)
    grad_norm_attn = jnp.sum(grad_act_one * inputs * factor_one, axis=0)
    grad_inputs = grad_middle + rms_back(inputs, factor_one, grad_act_one, norm_attn)

    small = (
        grad_norm_attn,
        gain_sums[0, :HALF] + gain_sums[0, HALF:],
        gain_sums[1, :HALF] + gain_sums[1, HALF:],
        bias_sums[0, :heads],
    )
    (own_proj,), small = reduce_all(mesh, (grad_proj,), small, 4, True)
    return (
        result[None],
        grad_inputs[None],
        own_proj[:, : 3 * width],
        own_proj[:, 4 * width : 4 * width + heads],
        own_proj[:, 3 * width : 4 * width],
        own_out,
        own_gu,
        own_down,
        small[0],
        sum_norm_ffn,
        small[1],
        small[2],
        small[3],
        sum_ogate_bias,
    )


def solution(mesh):
    block = P(("dp", "fsdp"), "ctx", None)
    rows = P("fsdp", None)
    return jax.shard_map(
        functools.partial(shards, mesh),
        mesh=mesh,
        in_specs=(block, block) + (rows,) * 6 + (P(),) * 6,
        out_specs=(block, block) + (rows,) * 6 + (P(),) * 6,
        check_vma=False,
    )
```
